512 devices in a mesh: dp: 8 (over x, core), expert: 64 (over z, y).
Axes of the slice: x: 4, y: 8, z: 8, core: 2. Of those that a mesh axis runs over, the one named last changes fastest.
Arguments:
- query_reps: bfloat16 [4096, 2048], P('dp'), as said below
- code_reps: bfloat16 [4096, 2048], P('expert'), as said below
- positives: int32 [4096], P('dp'), may hold values from 0 to 4095, as said below
- file_lengths: int32 [64, 8, 8], P('expert', 'dp'), may hold values from 1 to 64, 128 in all within a row
- residual: bfloat16 [64, 1024, 2048], P('expert', 'dp'), may hold values from -6 to 6
- norm_gain: bfloat16 [2048], replicated, may hold values from 0.25 to 1.75
- expert_ids: int32 [64, 1024, 2], P('expert', 'dp'), may hold values from 0 to 63, as said below
- gate_units: int32 [64, 1024, 2], P('expert', 'dp'), may hold values from 16 to 191
- w_gate: bfloat16 [64, 2048, 768], P('expert', 'dp'), may hold values from -0.125 to 0.125
- w_up: bfloat16 [64, 2048, 768], P('expert', 'dp'), may hold values from -0.125 to 0.125
- w_down: bfloat16 [64, 2048, 768], P('expert', 'dp'), may hold values from -0.21875 to 0.21875
Outputs:
- token_grad: bfloat16 [64, 1024, 2048], P('expert', 'dp')
The draws below stay inside these ranges and needn't reach their ends.
Inputs may be any that keep to these rules, and one draw needn't show every extreme that they name: `positives`: each code is the positive of exactly one query. `query_reps`: entries have magnitude at most 4 / sqrt(2048). `code_reps`: entries have magnitude at most 4 / sqrt(2048). `file_lengths`: the 8 lengths of one shard add up to 128. `expert_ids`: each token names 2 different experts; the tokens of one shard name each expert at most 6 times, and for each index of dp some expert is named exactly 6 times by the tokens of every shard with that index.
All inputs are finite; a program needn't handle non-finite values.
Results may differ from the reference program's by a relative error of at most 0.009.
Values may be sent and summed in bfloat16 or wider, within the bound.
No kernel may reach another device: no remote copies, remote signals or barrier semaphores. Data moves between devices by JAX's collectives and lax.ppermute only.
A program may use at most 64 MiB of HBM per device.

```python
import math
import jax
import jax.numpy as jnp
import numpy as np
from jax import lax

D = 2048
FF = 768
TOK_DEV = 128
TOP = 2
EXPERTS = 64
SHARDS = 8
FILES_DEV = 8
MOSTLEN = 64
CAP = 6
FILES = 4096


RHO = 0.45


NOISE_WEIGHT = 0.89


def shared_reps(key):
    file_total = FILES
    spread = D ** (-0.5)
    key_pos = jax.random.fold_in(key, 11)
    key_code = jax.random.fold_in(key, 12)
    key_noise = jax.random.fold_in(key, 13)
    positives = jax.random.permutation(key_pos, file_total).astype(jnp.int32)
    codes = jax.random.truncated_normal(key_code, -3.0, 3.0, (file_total, D), jnp.float32)
    noise = jax.random.truncated_normal(key_noise, -3.0, 3.0, (file_total, D), jnp.float32)
    queries = RHO * codes[positives] + NOISE_WEIGHT * noise
    codes = jnp.clip(codes, -4.0, 4.0) * spread
    queries = jnp.clip(queries, -4.0, 4.0) * spread
    return (positives, codes, queries)


def draw_positives(key, part):
    return shared_reps(key)[0]


def draw_code_reps(key, part):
    return shared_reps(key)[1].astype(jnp.bfloat16)


def draw_query_reps(key, part):
    return shared_reps(key)[2].astype(jnp.bfloat16)


def draw_expert_ids(key, part):
    slot_total = EXPERTS * CAP
    hot_expert = jax.random.randint(jax.random.fold_in(key, 21), (SHARDS,), 0, EXPERTS)

    def one_block(block):
        block_key = jax.random.fold_in(key, 1000 + block)
        key_score = jax.random.fold_in(block_key, 1)
        key_perm = jax.random.fold_in(block_key, 2)
        number = jnp.arange(slot_total, dtype=jnp.int32)
        slot_owner = number // CAP
        scores = jax.random.randint(key_score, (slot_total,), 0, 262144) * slot_total + number
        scores = jnp.where(slot_owner == hot_expert[block % SHARDS], number - slot_total, scores)
        ranking = jnp.argsort(scores)
        picked = jnp.sort(ranking[:TOK_DEV * TOP])
        pairs = (picked // CAP).reshape(TOP, TOK_DEV).T
        return pairs[jax.random.permutation(key_perm, TOK_DEV)]
    blocks = jax.vmap(one_block)(jnp.arange(EXPERTS * SHARDS, dtype=jnp.int32))
    return blocks.reshape(EXPERTS, SHARDS * TOK_DEV, TOP).astype(jnp.int32)


def with_ends(drawn, key, low, high):
    longest = drawn.shape.index(max(drawn.shape))
    spots = []
    for shift in (0, 1):
        where = [jax.random.randint(jax.random.fold_in(key, axis), (), 0, length) for axis, length in enumerate(drawn.shape)]
        where[longest] = (where[longest] + shift) % drawn.shape[longest]
        spots.append(tuple(where))
    return drawn.at[spots[0]].set(low).at[spots[1]].set(high)


def block_levels(stream_key, extent, pieces, low, top_value):
    level = 1.0
    for dim, blocks in pieces:
        heights = jax.random.uniform(jax.random.fold_in(jax.random.fold_in(stream_key, 6), dim), (blocks,), jnp.float32, low / len(pieces), top_value / len(pieces))
        level = level * jnp.repeat(jnp.exp(heights), extent[dim] // blocks).reshape((-1,) + (1,) * (len(extent) - 1 - dim))
    return level


def profile(count, total, bound, skew):
    portions = [(1 << 20) // math.isqrt(grade ** skew) + 1 for grade in range(2, count + 1)]
    surplus, holding = total - bound - (count - 1), [1] * (count - 1)
    while surplus > 0:
        free = [i for i in range(count - 1) if holding[i] < bound]
        whole, budget = sum([portions[i] for i in free]), surplus
        for i in free:
            more = min(bound - holding[i], max(1, budget * portions[i] // whole), surplus)
            holding[i] = holding[i] + more
            surplus = surplus - more
    return np.array([bound] + holding)


def ragged_sizes(own_key, number_of, total, limit, lean):
    if number_of == 2:
        one = jax.random.randint(own_key, (), max(1, total - limit), min(limit, total - 1) + 1)
        return jnp.stack([one, total - one])
    sizes = jnp.asarray(profile(number_of, total, limit, lean), jnp.int32)
    twos = (number_of - 1) // 2
    donor, taker = sizes[1:1 + 2 * twos:2], sizes[2:2 + 2 * twos:2]
    margin = jnp.minimum(donor - 1, limit - taker)
    passed = jax.random.randint(jax.random.fold_in(own_key, 1), (twos,), 0, 1 << 20) % (margin + 1)
    sizes = sizes.at[1:1 + 2 * twos:2].set(donor - passed).at[2:2 + 2 * twos:2].set(taker + passed)
    return sizes[jax.random.permutation(jax.random.fold_in(own_key, 2), number_of)]


def gaussian(rng, extent, scale, most, cuts=(), held_as=jnp.bfloat16):
    gain = block_levels(rng, extent, cuts, -0.22, 0.18) if cuts else 1.0
    drawn = jax.random.normal(rng, extent, jnp.float32) * scale * gain
    return jnp.minimum(jnp.maximum(drawn, -most), most).astype(held_as)


def setup_inputs(seed: int = 0) -> dict:
    splits = jax.random.split(jax.random.key(seed), 12)
    return {
        "query_reps": draw_query_reps(jax.random.fold_in(splits[11], 71), 0),
        "code_reps": draw_code_reps(jax.random.fold_in(splits[11], 71), 0),
        "positives": draw_positives(jax.random.fold_in(splits[11], 71), 0),
        "file_lengths": jax.vmap(lambda own: ragged_sizes(own, FILES_DEV, TOK_DEV, MOSTLEN, 2))(jax.random.split(splits[3], EXPERTS * SHARDS)).reshape((EXPERTS, SHARDS, FILES_DEV)).astype(jnp.int32),
        "residual": gaussian(splits[4], (EXPERTS, SHARDS * TOK_DEV, D), 1.0, 6.0, ((0, 64), (1, 8))),
        "norm_gain": jnp.clip(1.0 + 0.15 * jax.random.normal(splits[5], (D,), jnp.float32), 0.25, 1.75).astype(jnp.bfloat16),
        "expert_ids": draw_expert_ids(jax.random.fold_in(splits[11], 71), 0),
        "gate_units": with_ends(jax.random.randint(splits[7], (EXPERTS, SHARDS * TOK_DEV, TOP), 16, 192), jax.random.fold_in(splits[7], 1), 16, 191).astype(jnp.int32),
        "w_gate": gaussian(splits[8], (EXPERTS, D, FF), D ** -0.5, 0.125, ((0, 64), (1, 8))),
        "w_up": gaussian(splits[9], (EXPERTS, D, FF), D ** -0.5, 0.125, ((0, 64), (1, 8))),
        "w_down": gaussian(splits[10], (EXPERTS, D, FF), FF ** -0.5, 0.21875, ((0, 64), (1, 8))),
    }


SCORE_SCALE = 20.0
GRAD_SCALE = 2560.0
EPSILON = 1e-06

def expert_backward(normed_rows, cot_rows, gate_rows, weight_gate, weight_up, weight_down):
    gate_pre = jnp.dot(normed_rows, weight_gate, preferred_element_type=jnp.float32)
    up_pre = jnp.dot(normed_rows, weight_up, preferred_element_type=jnp.float32)
    back_hidden = gate_rows[:, None] * jnp.dot(cot_rows, weight_down, preferred_element_type=jnp.float32)
    sigmoid_gate = jax.nn.sigmoid(gate_pre)
    grad_gate = (back_hidden * up_pre * sigmoid_gate * (1.0 + gate_pre * (1.0 - sigmoid_gate))).astype(jnp.bfloat16)
    grad_up = (back_hidden * gate_pre * sigmoid_gate).astype(jnp.bfloat16)
    contract = (((1,), (1,)), ((), ()))
    input_grad = lax.dot_general(grad_gate, weight_gate, contract, preferred_element_type=jnp.float32)
    input_grad = input_grad + lax.dot_general(grad_up, weight_up, contract, preferred_element_type=jnp.float32)
    return input_grad.astype(jnp.bfloat16)

def reference(query_reps, code_reps, positives, file_lengths, residual, norm_gain, expert_ids, gate_units, w_gate, w_up, w_down):
    file_total = query_reps.shape[0]
    scores = jnp.dot(query_reps, code_reps.T, preferred_element_type=jnp.float32) * SCORE_SCALE
    row_top = lax.optimization_barrier(jnp.max(scores, axis=1, keepdims=True))
    exponent = jnp.exp(scores - row_top)
    probabilities = exponent / lax.optimization_barrier(jnp.sum(exponent, axis=1, keepdims=True))
    onehot = (positives[:, None] == jnp.arange(file_total, dtype=jnp.int32)[None, :]).astype(jnp.float32)
    weights = (GRAD_SCALE * (probabilities - onehot)).astype(jnp.bfloat16)
    code_grad = jnp.dot(weights.T, query_reps, preferred_element_type=jnp.float32)
    owners, seq_rows, model_width = residual.shape
    shard_count = file_lengths.shape[1]
    file_count = file_lengths.shape[2]
    tokens = seq_rows // shard_count
    lengths = file_lengths.astype(jnp.float32)
    file_cot = (code_grad.reshape(owners, shard_count, file_count, model_width) / lengths[..., None]).astype(jnp.bfloat16)
    file_ends = jnp.cumsum(file_lengths, axis=2).astype(jnp.int32)
    position = jnp.arange(tokens, dtype=jnp.int32)
    segment = lax.optimization_barrier(jnp.sum((position[None, None, :, None] >= file_ends[:, :, None, :]).astype(jnp.int32), axis=3)).astype(jnp.int32)
    block_base = jnp.arange(owners * shard_count, dtype=jnp.int32).reshape(owners, shard_count) * file_count
    file_index = (block_base[:, :, None] + segment).reshape(-1)
    token_cot = file_cot.reshape(-1, model_width)[file_index]
    stream = residual.astype(jnp.float32)
    root_inverse = lax.rsqrt(lax.optimization_barrier(jnp.mean(stream * stream, axis=-1, keepdims=True)) + EPSILON)
    norm_scale = norm_gain.astype(jnp.float32)
    normed = (stream * root_inverse * norm_scale).astype(jnp.bfloat16)
    token_count = owners * seq_rows
    flat_normed = normed.reshape(token_count, model_width)
    flat_ids = expert_ids.reshape(-1).astype(jnp.int32)
    gate_values = gate_units.reshape(-1).astype(jnp.float32) / 256.0
    count_total = flat_ids.shape[0]
    ranking = jnp.argsort(flat_ids, stable=True).astype(jnp.int32)
    counts = lax.optimization_barrier(jnp.sum((flat_ids[None, :] == jnp.arange(owners, dtype=jnp.int32)[:, None]).astype(jnp.int32), axis=1)).astype(jnp.int32)
    starts = (jnp.cumsum(counts) - counts).astype(jnp.int32)
    row_bound = CAP * SHARDS * EXPERTS
    padded_order = jnp.concatenate([ranking, jnp.full((row_bound,), count_total, jnp.int32)])
    normed_pad = jnp.concatenate([flat_normed, jnp.zeros((1, model_width), jnp.bfloat16)])
    cot_pad = jnp.concatenate([token_cot, jnp.zeros((1, model_width), jnp.bfloat16)])
    gate_pad = jnp.concatenate([gate_values, jnp.zeros((1,), jnp.float32)])

    def one_expert(carry, expert):
        picked = lax.dynamic_slice_in_dim(padded_order, starts[expert], row_bound)
        is_valid = jnp.arange(row_bound, dtype=jnp.int32) < counts[expert]
        picked = jnp.where(is_valid, picked, count_total).astype(jnp.int32)
        token_row = jnp.where(is_valid, picked // TOP, token_count).astype(jnp.int32)
        input_grad = expert_backward(normed_pad[token_row], cot_pad[token_row], gate_pad[picked], w_gate[expert], w_up[expert], w_down[expert])
        return (carry.at[token_row].add(input_grad.astype(jnp.float32)), None)
    normed_grad, _ = lax.scan(one_expert, jnp.zeros((token_count + 1, model_width), jnp.float32), jnp.arange(owners, dtype=jnp.int32))
    normed_grad = normed_grad[:token_count].reshape(owners, seq_rows, model_width)
    scaled = norm_scale * normed_grad
    correction = lax.optimization_barrier(jnp.mean(scaled * stream, axis=-1, keepdims=True))
    token_grad = token_cot.reshape(owners, seq_rows, model_width).astype(jnp.float32) + root_inverse * scaled - stream * root_inverse ** 3 * correction
    return token_grad.astype(jnp.bfloat16)
```

```python
import functools
import jax
import jax.numpy as jnp
from jax import lax
from jax.experimental import pallas as pl
from jax.experimental.pallas import tpu as pltpu
from jax.sharding import PartitionSpec as P

SCORE_SCALE = 20.0
GRAD_SCALE = 2560.0
EPSILON = 1e-06
BF = jnp.bfloat16
F32 = jnp.float32

SLOTS = 6
BLOCK = 8
SECTION = 512
SECTIONS = 3


def iota(shape, dim):
    return lax.broadcasted_iota(jnp.int32, shape, dim)


def dot(a, b):
    return jnp.dot(a, b, preferred_element_type=F32)


def dot_first(a, b):
    return lax.dot_general(a, b, (((0,), (0,)), ((), ())), preferred_element_type=F32)


def dot_last(a, b):
    return lax.dot_general(a, b, (((1,), (1,)), ((), ())), preferred_element_type=F32)


def section(k):
    return slice(k * SECTION, (k + 1) * SECTION)


def tail_row(q, k):
    rank = jnp.bitwise_and(q, BLOCK - 1)
    high = (rank >= 3).astype(jnp.int32)
    return jnp.where(rank - 3 * high == k, q - rank + SLOTS + high, -1)


def picks(rows, q, first, second):
    r = iota((rows, q.shape[1]), 0)
    zero = jnp.zeros((), F32)
    return (jnp.where(r == q[0:1], first, zero) + jnp.where(r == q[1:2], second, zero)).astype(BF)


def pack_rows(rows_ref, q, out_ref):
    total = out_ref.shape[0]
    main = picks(total, q, 1.0, 1.0)
    tail = rows_ref[:, section(SECTIONS)]
    for k in range(SECTIONS):
        left = jnp.concatenate([main, picks(total, tail_row(q, k), 1.0, 1.0)], axis=1)
        right = jnp.concatenate([rows_ref[:, section(k)], tail], axis=0)
        out_ref[:, section(k)] = dot(left, right).astype(BF)


def inverse_rms(stream):
    return lax.rsqrt(jnp.mean(stream * stream, axis=-1, keepdims=True) + EPSILON)


def dispatch_kernel(residual_ref, gain_ref, ids_ref, out_ref, q_ref, normed_ref, *, experts):
    stream = residual_ref[...].astype(F32)
    normed_ref[...] = (stream * inverse_rms(stream) * gain_ref[...].astype(F32)).astype(BF)
    ids = jnp.concatenate([ids_ref[0:1, :], ids_ref[1:2, :]], axis=1)
    count = ids.shape[1]
    table = (iota((experts, count), 0) == ids).astype(F32)
    earlier = dot(
        table.astype(BF), (iota((count, count), 0) < iota((count, count), 1)).astype(F32).astype(BF)
    )
    rank = jnp.sum(table * earlier, axis=0, keepdims=True).astype(jnp.int32)
    q_flat = ids * BLOCK + rank
    half = count // 2
    q = jnp.concatenate([q_flat[:, :half], q_flat[:, half:]], axis=0)
    q_ref[...] = q
    pack_rows(normed_ref, q, out_ref)


def file_cotangent(code_grad_ref, lengths_ref):
    files = code_grad_ref.shape[0]
    length = jnp.zeros((files, 1), jnp.int32)
    row = iota((files, 1), 0)
    for f in range(files):
        length = jnp.where(row == f, lengths_ref[0, f], length)
    return (code_grad_ref[...] / length.astype(F32)).astype(BF)


def token_cotangent(code_grad_ref, lengths_ref, tokens):
    files = code_grad_ref.shape[0]
    position = iota((1, tokens), 1)
    segment = jnp.zeros((1, tokens), jnp.int32)
    end = jnp.int32(0)
    for f in range(files):
        end = end + lengths_ref[0, f]
        segment = segment + (position >= end).astype(jnp.int32)
    member = (iota((files, tokens), 0) == segment).astype(F32).astype(BF)
    return dot_first(member, file_cotangent(code_grad_ref, lengths_ref))


def cotangent_kernel(code_grad_ref, lengths_ref, q_ref, out_ref, token_ref):
    token_ref[...] = token_cotangent(code_grad_ref, lengths_ref, token_ref.shape[0]).astype(BF)
    pack_rows(token_ref, q_ref[...], out_ref)


def halves(total):
    return 2 if total % 512 == 0 else 1


def unpack_blocks(block_ref, rows_ref):
    parts = halves(block_ref.shape[0])
    height = block_ref.shape[0] // parts
    wide = height // BLOCK * SLOTS
    i, r = iota((wide, height), 0), iota((wide, height), 1)
    peer, j = r >> 3, r & (BLOCK - 1)
    main = ((i == peer * SLOTS + j) & (j < SLOTS)).astype(F32).astype(BF)
    for g in range(parts):
        rows = slice(g * wide, (g + 1) * wide)
        tail = jnp.zeros((wide, SECTION), F32)
        for k in range(SECTIONS):
            last = ((i == peer * SLOTS + (j - SLOTS) * 3 + k) & (j >= SLOTS)).astype(F32).astype(BF)
            both = dot(
                jnp.concatenate([main, last], axis=0),
                block_ref[g * height : (g + 1) * height, section(k)],
            )
            rows_ref[rows, section(k)] = both[:wide].astype(BF)
            tail = tail + both[wide:]
        rows_ref[rows, section(SECTIONS)] = tail.astype(BF)


def pack_blocks(rows_ref, block_ref):
    parts = halves(block_ref.shape[0])
    height = block_ref.shape[0] // parts
    wide = height // BLOCK * SLOTS
    r, i = iota((height, wide), 0), iota((height, wide), 1)
    peer, j = r >> 3, r & (BLOCK - 1)
    main = ((i == peer * SLOTS + j) & (j < SLOTS)).astype(F32).astype(BF)
    for g in range(parts):
        rows = slice(g * wide, (g + 1) * wide)
        tail = rows_ref[rows, section(SECTIONS)].astype(BF)
        for k in range(SECTIONS):
            last = ((i == peer * SLOTS + (j - SLOTS) * 3 + k) & (j >= SLOTS)).astype(F32).astype(BF)
            block_ref[g * height : (g + 1) * height, section(k)] = (
                dot(main, rows_ref[rows, section(k)].astype(BF)) + dot(last, tail)
            ).astype(BF)


def forward_kernel(block_ref, gate_ref, up_ref, by_gate_ref, by_up_ref, rows_ref):
    @pl.when(pl.program_id(0) == 0)
    def _():
        unpack_blocks(block_ref, rows_ref)

    gate_pre = dot(rows_ref[...], gate_ref[...])
    up_pre = dot(rows_ref[...], up_ref[...])
    s = jax.nn.sigmoid(gate_pre)
    by_gate_ref[...] = up_pre * s * (1.0 + gate_pre * (1.0 - s))
    by_up_ref[...] = gate_pre * s


def backward_kernel(
    block_ref, down_ref, gate_ref, up_ref, by_gate_ref, by_up_ref, out_ref, rows_ref, total_ref
):
    step = pl.program_id(0)

    @pl.when(step == 0)
    def _():
        unpack_blocks(block_ref, rows_ref)

    back = dot(rows_ref[...], down_ref[...])
    part = dot_last((back * by_gate_ref[...]).astype(BF), gate_ref[...]) + dot_last(
        (back * by_up_ref[...]).astype(BF), up_ref[...]
    )

    @pl.when(step == 0)
    def _():
        total_ref[...] = part

    @pl.when(step > 0)
    def _():
        total_ref[...] += part

    @pl.when(step == pl.num_programs(0) - 1)
    def _():
        pack_blocks(total_ref, out_ref)


def finish_kernel(
    block_ref, residual_ref, gain_ref, q_ref, units_ref, code_grad_ref, lengths_ref, out_ref, grad_ref
):
    total, q = block_ref.shape[0], q_ref[...]
    gates = units_ref[...].astype(F32) * (1.0 / 256.0)
    first, second = gates[0:1], gates[1:2]
    tokens = q.shape[1]
    main = picks(total, q, first, second)
    tail = jnp.zeros((tokens, SECTION), F32)
    for k in range(SECTIONS):
        both = dot_first(
            jnp.concatenate([main, picks(total, tail_row(q, k), first, second)], axis=1),
            block_ref[:, section(k)],
        )
        grad_ref[:, section(k)] = both[:tokens]
        tail = tail + both[tokens:]
    grad_ref[:, section(SECTIONS)] = tail
    stream = residual_ref[...].astype(F32)
    root = inverse_rms(stream)
    scaled = gain_ref[...].astype(F32) * grad_ref[...]
    correction = jnp.mean(scaled * stream, axis=-1, keepdims=True)
    cot = token_cotangent(code_grad_ref, lengths_ref, tokens)
    out_ref[...] = (cot + root * scaled - stream * (root * root * root * correction)).astype(BF)


PARAMS = pltpu.CompilerParams(vmem_limit_bytes=56 << 20)
IN_SMEM = pl.BlockSpec(memory_space=pltpu.SMEM)
IN_VMEM = pl.BlockSpec(memory_space=pltpu.VMEM)


def halve_over_dp(rows, files):
    me = lax.axis_index("dp")
    size = lax.axis_size("dp")
    value = rows.reshape(size, files, rows.shape[1])
    bit = 1
    while bit < size:
        value = value.reshape(value.shape[0] // 2, 2, files, rows.shape[1])
        mine = (me // bit) % 2
        keep = lax.dynamic_index_in_dim(value, mine, 1, keepdims=False)
        give = lax.dynamic_index_in_dim(value, 1 - mine, 1, keepdims=False)
        value = keep + lax.ppermute(give, "dp", [(d, d ^ bit) for d in range(size)])
        bit *= 2
    return value.reshape(files, rows.shape[1])


def per_device(
    query_reps,
    code_reps,
    positives,
    file_lengths,
    residual,
    norm_gain,
    expert_ids,
    gate_units,
    w_gate,
    w_up,
    w_down,
):
    owners = lax.axis_size("expert")
    columns = code_reps.shape[0]
    queries, width = query_reps.shape
    files = file_lengths.shape[2]
    tokens = residual.shape[1]
    hidden = w_gate.shape[2]
    total = owners * BLOCK
    lengths = file_lengths.reshape(1, files)
    stream = residual[0]
    gain = norm_gain.reshape(1, width)
    ids = expert_ids[0].T
    units = gate_units[0].T

    weights = lax.all_gather(
        jnp.concatenate([w_gate[0], w_up[0], w_down[0]], axis=1), "dp", axis=0, tiled=True
    )

    scores = dot_last(code_reps, query_reps) * SCORE_SCALE
    local_top = jnp.max(scores, axis=0)
    local_total = jnp.sum(jnp.exp(scores - local_top[None, :]), axis=0)
    stats = jnp.concatenate([local_top, local_total])
    stats = lax.all_to_all(
        jnp.broadcast_to(stats[None, None], (owners, 1, 2 * queries)), "expert", 0, 0, tiled=True
    ).reshape(owners, 2 * queries)
    tops, totals = stats[:, :queries], stats[:, queries:]
    row_top = jnp.max(tops, axis=0)
    row_total = jnp.sum(totals * jnp.exp(tops - row_top[None, :]), axis=0)
    probabilities = jnp.exp(scores - row_top[None, :]) / row_total[None, :]
    column_ids = lax.axis_index("expert") * columns + jnp.arange(columns, dtype=jnp.int32)
    onehot = (positives[None, :] == column_ids[:, None]).astype(F32)
    code_weights = (GRAD_SCALE * (probabilities - onehot)).astype(BF)
    code_grad = halve_over_dp(dot(code_weights, query_reps), files)

    blocks, q = pl.pallas_call(
        functools.partial(dispatch_kernel, experts=owners),
        out_shape=(
            jax.ShapeDtypeStruct((total, SECTIONS * SECTION), BF),
            jax.ShapeDtypeStruct((2, tokens), jnp.int32),
        ),
        in_specs=[IN_VMEM] * 3,
        out_specs=(IN_VMEM, IN_VMEM),
        scratch_shapes=[pltpu.VMEM((tokens, width), BF)],
        compiler_params=PARAMS,
        name="dispatch",
    )(stream, gain, ids)

    def exchange(value):
        shape = value.shape
        return lax.all_to_all(
            value.reshape(owners, BLOCK, shape[1]), "expert", 0, 0, tiled=True
        ).reshape(shape)

    blocks = exchange(blocks)
    cot_blocks = exchange(
        pl.pallas_call(
            cotangent_kernel,
            out_shape=jax.ShapeDtypeStruct((total, SECTIONS * SECTION), BF),
            in_specs=[IN_VMEM, IN_SMEM, IN_VMEM],
            out_specs=IN_VMEM,
            scratch_shapes=[pltpu.VMEM((tokens, width), BF)],
            compiler_params=PARAMS,
            name="cotangent",
        )(code_grad, lengths, q)
    )

    step = 256
    steps = hidden // step
    rows = owners * SLOTS
    whole = pl.BlockSpec((total, SECTIONS * SECTION), lambda f: (0, 0), pipeline_mode=pl.Buffered(1))
    part = pl.BlockSpec((rows, step), lambda f: (0, f))
    gate_part = pl.BlockSpec((width, step), lambda f: (0, f))
    up_part = pl.BlockSpec((width, step), lambda f: (0, steps + f))
    down_part = pl.BlockSpec((width, step), lambda f: (0, 2 * steps + f))
    by_gate, by_up = pl.pallas_call(
        forward_kernel,
        out_shape=(jax.ShapeDtypeStruct((rows, hidden), F32),) * 2,
        grid=(steps,),
        in_specs=[whole, gate_part, up_part],
        out_specs=(part, part),
        scratch_shapes=[pltpu.VMEM((rows, width), BF)],
        compiler_params=PARAMS,
        name="expert_forward",
    )(blocks, weights, weights)
    result = pl.pallas_call(
        backward_kernel,
        out_shape=jax.ShapeDtypeStruct((total, SECTIONS * SECTION), BF),
        grid=(steps,),
        in_specs=[whole, down_part, gate_part, up_part, part, part],
        out_specs=whole,
        scratch_shapes=[pltpu.VMEM((rows, width), BF), pltpu.VMEM((rows, width), F32)],
        compiler_params=PARAMS,
        name="expert_backward",
    )(cot_blocks, weights, weights, weights, by_gate, by_up)

    token_grad = pl.pallas_call(
        finish_kernel,
        out_shape=jax.ShapeDtypeStruct((tokens, width), BF),
        in_specs=[IN_VMEM] * 6 + [IN_SMEM],
        out_specs=IN_VMEM,
        scratch_shapes=[pltpu.VMEM((tokens, width), F32)],
        compiler_params=PARAMS,
        name="finish",
    )(exchange(result), stream, gain, q, units, code_grad, lengths)
    return token_grad[None]


def solution(mesh):
    return jax.shard_map(
        per_device,
        mesh=mesh,
        in_specs=(
            P("dp", None),
            P("expert", None),
            P("dp"),
            P("expert", "dp", None),
            P("expert", "dp", None),
            P(),
            P("expert", "dp", None),
            P("expert", "dp", None),
            P("expert", "dp", None),
            P("expert", "dp", None),
            P("expert", "dp", None),
        ),
        out_specs=P("expert", "dp", None),
        check_vma=False,
    )
```

```python
import functools
import jax
import jax.numpy as jnp
from jax import lax
from jax.experimental import pallas as pl
from jax.experimental.pallas import tpu as pltpu
from jax.sharding import PartitionSpec as P

SCORE_SCALE = 20.0
GRAD_SCALE = 2560.0
EPSILON = 1e-06
BF = jnp.bfloat16
F32 = jnp.float32

SLOTS = 6
BLOCK = 8
SECTION = 512
SECTIONS = 3


def iota(shape, dim):
    return lax.broadcasted_iota(jnp.int32, shape, dim)


def dot(a, b):
    return jnp.dot(a, b, preferred_element_type=F32)


def dot_first(a, b):
    return lax.dot_general(a, b, (((0,), (0,)), ((), ())), preferred_element_type=F32)


def dot_last(a, b):
    return lax.dot_general(a, b, (((1,), (1,)), ((), ())), preferred_element_type=F32)


def section(k):
    return slice(k * SECTION, (k + 1) * SECTION)


def tail_row(q, k):
    rank = jnp.bitwise_and(q, BLOCK - 1)
    high = (rank >= 3).astype(jnp.int32)
    return jnp.where(rank - 3 * high == k, q - rank + SLOTS + high, -1)


def picks(rows, q, first, second):
    r = iota((rows, q.shape[1]), 0)
    zero = jnp.zeros((), F32)
    return (jnp.where(r == q[0:1], first, zero) + jnp.where(r == q[1:2], second, zero)).astype(BF)


def pack_rows(rows_ref, q, out_ref):
    total = out_ref.shape[0]
    main = picks(total, q, 1.0, 1.0)
    tail = rows_ref[:, section(SECTIONS)]
    for k in range(SECTIONS):
        left = jnp.concatenate([main, picks(total, tail_row(q, k), 1.0, 1.0)], axis=1)
        right = jnp.concatenate([rows_ref[:, section(k)], tail], axis=0)
        out_ref[:, section(k)] = dot(left, right).astype(BF)


def inverse_rms(stream):
    return lax.rsqrt(jnp.mean(stream * stream, axis=-1, keepdims=True) + EPSILON)


def dispatch_kernel(
    residual_ref, gain_ref, ids_ref, w0_ref, w1_ref, w2_ref, out_ref, q_ref, joined_ref, normed_ref, sems, *, experts
):
    hidden = w0_ref.shape[1]
    copies = [
        pltpu.make_async_copy(w_ref, joined_ref.at[:, k * hidden : (k + 1) * hidden], sems.at[k])
        for k, w_ref in enumerate((w0_ref, w1_ref, w2_ref))
    ]
    for copy in copies:
        copy.start()
    stream = residual_ref[...].astype(F32)
    normed_ref[...] = (stream * inverse_rms(stream) * gain_ref[...].astype(F32)).astype(BF)
    ids = jnp.concatenate([ids_ref[0:1, :], ids_ref[1:2, :]], axis=1)
    count = ids.shape[1]
    table = (iota((experts, count), 0) == ids).astype(F32)
    earlier = dot(
        table.astype(BF), (iota((count, count), 0) < iota((count, count), 1)).astype(F32).astype(BF)
    )
    rank = jnp.sum(table * earlier, axis=0, keepdims=True).astype(jnp.int32)
    q_flat = ids * BLOCK + rank
    half = count // 2
    q = jnp.concatenate([q_flat[:, :half], q_flat[:, half:]], axis=0)
    q_ref[...] = q
    pack_rows(normed_ref, q, out_ref)
    for copy in copies:
        copy.wait()


def file_cotangent(code_grad_ref, lengths_ref):
    files = code_grad_ref.shape[0]
    length = jnp.zeros((files, 1), jnp.int32)
    row = iota((files, 1), 0)
    for f in range(files):
        length = jnp.where(row == f, lengths_ref[0, f], length)
    return (code_grad_ref[...] / length.astype(F32)).astype(BF)


def token_cotangent(code_grad_ref, lengths_ref, tokens):
    files = code_grad_ref.shape[0]
    position = iota((1, tokens), 1)
    segment = jnp.zeros((1, tokens), jnp.int32)
    end = jnp.int32(0)
    for f in range(files):
        end = end + lengths_ref[0, f]
        segment = segment + (position >= end).astype(jnp.int32)
    member = (iota((files, tokens), 0) == segment).astype(F32).astype(BF)
    return dot_first(member, file_cotangent(code_grad_ref, lengths_ref))


def cotangent_kernel(code_grad_ref, lengths_ref, q_ref, out_ref, token_ref):
    token_ref[...] = token_cotangent(code_grad_ref, lengths_ref, token_ref.shape[0]).astype(BF)
    pack_rows(token_ref, q_ref[...], out_ref)


def halves(total):
    return 2 if total % 512 == 0 else 1


def unpack_blocks(block_ref, rows_ref):
    parts = halves(block_ref.shape[0])
    height = block_ref.shape[0] // parts
    wide = height // BLOCK * SLOTS
    i, r = iota((wide, height), 0), iota((wide, height), 1)
    peer, j = r >> 3, r & (BLOCK - 1)
    main = ((i == peer * SLOTS + j) & (j < SLOTS)).astype(F32).astype(BF)
    for g in range(parts):
        rows = slice(g * wide, (g + 1) * wide)
        tail = jnp.zeros((wide, SECTION), F32)
        for k in range(SECTIONS):
            last = ((i == peer * SLOTS + (j - SLOTS) * 3 + k) & (j >= SLOTS)).astype(F32).astype(BF)
            both = dot(
                jnp.concatenate([main, last], axis=0),
                block_ref[g * height : (g + 1) * height, section(k)],
            )
            rows_ref[rows, section(k)] = both[:wide].astype(BF)
            tail = tail + both[wide:]
        rows_ref[rows, section(SECTIONS)] = tail.astype(BF)


def pack_blocks(rows_ref, block_ref):
    parts = halves(block_ref.shape[0])
    height = block_ref.shape[0] // parts
    wide = height // BLOCK * SLOTS
    r, i = iota((height, wide), 0), iota((height, wide), 1)
    peer, j = r >> 3, r & (BLOCK - 1)
    main = ((i == peer * SLOTS + j) & (j < SLOTS)).astype(F32).astype(BF)
    for g in range(parts):
        rows = slice(g * wide, (g + 1) * wide)
        tail = rows_ref[rows, section(SECTIONS)]
        for k in range(SECTIONS):
            last = ((i == peer * SLOTS + (j - SLOTS) * 3 + k) & (j >= SLOTS)).astype(F32).astype(BF)
            block_ref[g * height : (g + 1) * height, section(k)] = (
                dot(main, rows_ref[rows, section(k)]) + dot(last, tail)
            ).astype(BF)


def forward_kernel(block_ref, weights_ref, factor_ref, rows_ref):
    hidden = factor_ref.shape[1] // 2
    unpack_blocks(block_ref, rows_ref)
    gate_pre = dot(rows_ref[...], weights_ref[:, :hidden])
    up_pre = dot(rows_ref[...], weights_ref[:, hidden : 2 * hidden])
    s = jax.nn.sigmoid(gate_pre)
    factor_ref[:, :hidden] = up_pre * s * (1.0 + gate_pre * (1.0 - s))
    factor_ref[:, hidden:] = gate_pre * s


def backward_kernel(
    block_hbm, weights_hbm, factor_hbm, out_ref, block_ref, weights_ref, factor_ref, rows_ref, hidden_ref, sems
):
    hidden = factor_ref.shape[1] // 2
    parts = halves(block_ref.shape[0])
    height = block_ref.shape[0] // parts
    pieces = [(block_hbm, block_ref, (slice(g * height, (g + 1) * height), slice(None))) for g in range(parts)]
    pieces.append((weights_hbm, weights_ref, (slice(None), slice(2 * hidden, 3 * hidden))))
    pieces.append((factor_hbm, factor_ref, (slice(None), slice(None))))
    for k in range(SECTIONS + 1):
        pieces.append((weights_hbm, weights_ref, (section(k), slice(0, 2 * hidden))))
    copies = [
        pltpu.make_async_copy(source.at[at], target.at[at], sems.at[n])
        for n, (source, target, at) in enumerate(pieces)
    ]
    for copy in copies:
        copy.start()
    for copy in copies[:parts]:
        copy.wait()
    unpack_blocks(block_ref, rows_ref)
    copies[parts].wait()
    back = dot(rows_ref[...], weights_ref[:, 2 * hidden :])
    copies[parts + 1].wait()
    hidden_ref[:, :hidden] = (back * factor_ref[:, :hidden]).astype(BF)
    hidden_ref[:, hidden:] = (back * factor_ref[:, hidden:]).astype(BF)
    for k in range(SECTIONS + 1):
        copies[parts + 2 + k].wait()
        rows_ref[:, section(k)] = dot_last(
            hidden_ref[...], weights_ref[section(k), : 2 * hidden]
        ).astype(BF)
    pack_blocks(rows_ref, out_ref)


def finish_kernel(
    block_ref, residual_ref, gain_ref, q_ref, units_ref, code_grad_ref, lengths_ref, out_ref, grad_ref
):
    total, q = block_ref.shape[0], q_ref[...]
    gates = units_ref[...].astype(F32) * (1.0 / 256.0)
    first, second = gates[0:1], gates[1:2]
    tokens = q.shape[1]
    main = picks(total, q, first, second)
    tail = jnp.zeros((tokens, SECTION), F32)
    for k in range(SECTIONS):
        both = dot_first(
            jnp.concatenate([main, picks(total, tail_row(q, k), first, second)], axis=1),
            block_ref[:, section(k)],
        )
        grad_ref[:, section(k)] = both[:tokens]
        tail = tail + both[tokens:]
    grad_ref[:, section(SECTIONS)] = tail
    stream = residual_ref[...].astype(F32)
    root = inverse_rms(stream)
    scaled = gain_ref[...].astype(F32) * grad_ref[...]
    correction = jnp.mean(scaled * stream, axis=-1, keepdims=True)
    cot = token_cotangent(code_grad_ref, lengths_ref, tokens)
    out_ref[...] = (cot + root * scaled - stream * (root * root * root * correction)).astype(BF)


def params(mib):
    return pltpu.CompilerParams(vmem_limit_bytes=mib << 20)


IN_SMEM = pl.BlockSpec(memory_space=pltpu.SMEM)
IN_VMEM = pl.BlockSpec(memory_space=pltpu.VMEM)
IN_HBM = pl.BlockSpec(memory_space=pltpu.HBM)


def hbm(value):
    return pltpu.with_memory_space_constraint(value, pltpu.HBM)


def halve_over_dp(rows, files):
    me = lax.axis_index("dp")
    size = lax.axis_size("dp")
    value = rows.reshape(size, files, rows.shape[1])
    bit = 1
    while bit < size:
        value = value.reshape(value.shape[0] // 2, 2, files, rows.shape[1])
        mine = jnp.minimum(me & bit, 1)
        keep = lax.dynamic_index_in_dim(value, mine, 1, keepdims=False)
        give = lax.dynamic_index_in_dim(value, 1 - mine, 1, keepdims=False)
        value = keep + lax.ppermute(give, "dp", [(d, d ^ bit) for d in range(size)])
        bit *= 2
    return value.reshape(files, rows.shape[1])


def per_device(
    query_reps,
    code_reps,
    positives,
    file_lengths,
    residual,
    norm_gain,
    expert_ids,
    gate_units,
    w_gate,
    w_up,
    w_down,
):
    owners = lax.axis_size("expert")
    columns = code_reps.shape[0]
    queries, width = query_reps.shape
    files = file_lengths.shape[2]
    tokens = residual.shape[1]
    hidden = w_gate.shape[2]
    total = owners * BLOCK
    lengths = file_lengths.reshape(1, files)
    stream = residual[0]
    gain = norm_gain.reshape(1, width)
    ids = expert_ids[0].T
    units = gate_units[0].T

    blocks, q, joined = pl.pallas_call(
        functools.partial(dispatch_kernel, experts=owners),
        out_shape=(
            jax.ShapeDtypeStruct((total, SECTIONS * SECTION), BF),
            jax.ShapeDtypeStruct((2, tokens), jnp.int32),
            jax.ShapeDtypeStruct((w_gate.shape[1], 3 * hidden), BF),
        ),
        in_specs=[IN_VMEM] * 3 + [IN_HBM] * 3,
        out_specs=(IN_VMEM, IN_VMEM, IN_HBM),
        scratch_shapes=[pltpu.VMEM((tokens, width), BF), pltpu.SemaphoreType.DMA((3,))],
        compiler_params=params(12),
        name="dispatch",
    )(stream, gain, ids, hbm(w_gate[0]), hbm(w_up[0]), hbm(w_down[0]))
    scores = dot_last(code_reps, query_reps) * SCORE_SCALE
    owner = lax.axis_index("expert")
    column_ids = owner * columns + jnp.arange(columns, dtype=jnp.int32)
    positive = positives[None, :] == column_ids[:, None]
    local_top = jnp.max(scores, axis=0)
    exponent = jnp.exp(scores - local_top[None, :])
    local_rest = jnp.sum(jnp.where(positive, 0.0, exponent), axis=0)
    local_sum = local_top + jnp.log(jnp.sum(exponent, axis=0))
    sent = jnp.broadcast_to(local_sum[None, None], (owners, 1, queries))
    sums = lax.all_to_all(sent, "expert", 0, 0, tiled=True).reshape(owners, queries)
    sums, joined = lax.optimization_barrier((sums, joined))
    weights = lax.all_gather(joined, "dp", axis=0, tiled=True)
    row_top = jnp.max(sums, axis=0)
    shares = jnp.exp(sums - row_top[None, :])
    row_total = jnp.sum(shares, axis=0)
    own = (jnp.arange(owners, dtype=jnp.int32) == owner)[:, None]
    row_rest = jnp.sum(jnp.where(own, 0.0, shares), axis=0) + local_rest * jnp.exp(local_top - row_top)
    part = jnp.where(positive, -row_rest[None, :], jnp.exp(scores - row_top[None, :]))
    code_weights = (GRAD_SCALE * (part / row_total[None, :])).astype(BF)
    code_grad = halve_over_dp(dot(code_weights, query_reps), files)

    def exchange(value):
        shape = value.shape
        return lax.all_to_all(
            value.reshape(owners, BLOCK, shape[1]), "expert", 0, 0, tiled=True
        ).reshape(shape)

    blocks = exchange(blocks)
    cot_blocks = exchange(
        pl.pallas_call(
            cotangent_kernel,
            out_shape=jax.ShapeDtypeStruct((total, SECTIONS * SECTION), BF),
            in_specs=[IN_VMEM, IN_SMEM, IN_VMEM],
            out_specs=IN_VMEM,
            scratch_shapes=[pltpu.VMEM((tokens, width), BF)],
            compiler_params=params(12),
            name="cotangent",
        )(code_grad, lengths, q)
    )

    rows = owners * SLOTS
    factor = pl.pallas_call(
        forward_kernel,
        out_shape=jax.ShapeDtypeStruct((rows, 2 * hidden), F32),
        in_specs=[IN_VMEM] * 2,
        out_specs=IN_VMEM,
        scratch_shapes=[pltpu.VMEM((rows, width), BF)],
        compiler_params=params(16),
        name="expert_forward",
    )(blocks, weights)
    result = pl.pallas_call(
        backward_kernel,
        out_shape=jax.ShapeDtypeStruct((total, SECTIONS * SECTION), BF),
        in_specs=[IN_HBM] * 3,
        out_specs=IN_VMEM,
        scratch_shapes=[
            pltpu.VMEM((total, SECTIONS * SECTION), BF),
            pltpu.VMEM((width, 3 * hidden), BF),
            pltpu.VMEM((rows, 2 * hidden), F32),
            pltpu.VMEM((rows, width), BF),
            pltpu.VMEM((rows, 2 * hidden), BF),
            pltpu.SemaphoreType.DMA((halves(total) + SECTIONS + 3,)),
        ],
        compiler_params=params(32),
        name="expert_backward",
    )(hbm(cot_blocks), hbm(weights), hbm(factor))

    token_grad = pl.pallas_call(
        finish_kernel,
        out_shape=jax.ShapeDtypeStruct((tokens, width), BF),
        in_specs=[IN_VMEM] * 6 + [IN_SMEM],
        out_specs=IN_VMEM,
        scratch_shapes=[pltpu.VMEM((tokens, width), F32)],
        compiler_params=params(12),
        name="finish",
    )(exchange(result), stream, gain, q, units, code_grad, lengths)
    return token_grad[None]


def solution(mesh):
    return jax.shard_map(
        per_device,
        mesh=mesh,
        in_specs=(
            P("dp", None),
            P("expert", None),
            P("dp"),
            P("expert", "dp", None),
            P("expert", "dp", None),
            P(),
            P("expert", "dp", None),
            P("expert", "dp", None),
            P("expert", "dp", None),
            P("expert", "dp", None),
            P("expert", "dp", None),
        ),
        out_specs=P("expert", "dp", None),
        check_vma=False,
    )
```

```python
import functools
import jax
import jax.numpy as jnp
from jax import lax
from jax.experimental import pallas as pl
from jax.experimental.pallas import tpu as pltpu
from jax.sharding import PartitionSpec as P

SCORE_SCALE = 20.0
GRAD_SCALE = 2560.0
EPSILON = 1e-06
BF = jnp.bfloat16
F32 = jnp.float32

SLOTS = 6
BLOCK = 8
SECTION = 512
SECTIONS = 3
BLOCK_WIDTH = SECTIONS * SECTION
LANES = 128
PIECES = 4


def iota(shape, dim):
    return lax.broadcasted_iota(jnp.int32, shape, dim)


def dot(a, b):
    return jnp.dot(a, b, preferred_element_type=F32)


def dot_first(a, b):
    return lax.dot_general(a, b, (((0,), (0,)), ((), ())), preferred_element_type=F32)


def dot_last(a, b):
    return lax.dot_general(a, b, (((1,), (1,)), ((), ())), preferred_element_type=F32)


def section(k):
    return slice(k * SECTION, (k + 1) * SECTION)


def tail_row(q, k):
    rank = jnp.bitwise_and(q, BLOCK - 1)
    high = (rank >= 3).astype(jnp.int32)
    return jnp.where(rank - 3 * high == k, q - rank + SLOTS + high, -1)


def picks(rows, q, first, second):
    r = iota((rows, q.shape[1]), 0)
    zero = jnp.zeros((), F32)
    return (jnp.where(r == q[0:1], first, zero) + jnp.where(r == q[1:2], second, zero)).astype(BF)


def pack_rows(rows_ref, q, stage_ref, out_hbm, sems):
    total = stage_ref.shape[0]
    main = picks(total, q, 1.0, 1.0)
    tail = rows_ref[:, section(SECTIONS)]
    copies = []
    for k in range(SECTIONS):
        left = jnp.concatenate([main, picks(total, tail_row(q, k), 1.0, 1.0)], axis=1)
        right = jnp.concatenate([rows_ref[:, section(k)], tail], axis=0)
        stage_ref[:, section(k)] = dot(left, right).astype(BF)
        copies.append(
            pltpu.make_async_copy(stage_ref.at[:, section(k)], out_hbm.at[:, section(k)], sems.at[k])
        )
        copies[-1].start()
    return copies


def inverse_rms(stream):
    return lax.rsqrt(jnp.mean(stream * stream, axis=-1, keepdims=True) + EPSILON)


def dispatch_kernel(
    owner_ref,
    residual_ref,
    gain_ref,
    ids_ref,
    code_ref,
    positives_ref,
    query_hbm,
    w0_hbm,
    w1_hbm,
    w2_hbm,
    out_hbm,
    scores_hbm,
    q_ref,
    top_ref,
    rest_ref,
    joined_ref,
    query_ref,
    scores_ref,
    normed_ref,
    stage_ref,
    sems,
    *,
    experts,
):
    hidden, columns = w0_hbm.shape[1], code_ref.shape[0]
    parts = [slice(c * LANES, (c + 1) * LANES) for c in range(PIECES)]
    queries = [
        pltpu.make_async_copy(query_hbm.at[part], query_ref.at[part], sems.at[c])
        for c, part in enumerate(parts)
    ]
    for copy in queries:
        copy.start()
    copies = [
        pltpu.make_async_copy(w_hbm, joined_ref.at[:, k * hidden : (k + 1) * hidden], sems.at[PIECES + k])
        for k, w_hbm in enumerate((w0_hbm, w1_hbm, w2_hbm))
    ]
    for copy in copies:
        copy.start()
    stream = residual_ref[...].astype(F32)
    normed_ref[...] = (stream * inverse_rms(stream) * gain_ref[...].astype(F32)).astype(BF)
    ids = jnp.concatenate([ids_ref[0:1, :], ids_ref[1:2, :]], axis=1)
    count = ids.shape[1]
    table = (iota((experts, count), 0) == ids).astype(F32)
    earlier = dot(
        table.astype(BF), (iota((count, count), 0) < iota((count, count), 1)).astype(F32).astype(BF)
    )
    rank = jnp.sum(table * earlier, axis=0, keepdims=True).astype(jnp.int32)
    q_flat = ids * BLOCK + rank
    half = count // 2
    q = jnp.concatenate([q_flat[:, :half], q_flat[:, half:]], axis=0)
    q_ref[...] = q
    copies += pack_rows(normed_ref, q, stage_ref, out_hbm, sems.at[PIECES + 3 : PIECES + 3 + SECTIONS])
    column = owner_ref[0] * columns + iota((columns, 1), 0)
    high, low = [], []
    for copy, part in zip(queries, parts):
        copy.wait()
        scores = dot_last(code_ref[...], query_ref[part, :]) * SCORE_SCALE
        scores_ref[:, part] = scores
        top = jnp.max(scores, axis=0, keepdims=True)
        exponent = jnp.exp(scores - top)
        top_ref[:, part] = top
        rest_ref[:, part] = jnp.sum(
            jnp.where(positives_ref[:, part] == column, 0.0, exponent), axis=0, keepdims=True
        )
        log_sum = top + jnp.log(jnp.sum(exponent, axis=0, keepdims=True))
        high.append(log_sum.astype(BF).astype(F32))
        low.append(log_sum - high[-1])
    pieces = jnp.concatenate(high + low, axis=0)
    stage_ref[:, BLOCK_WIDTH:] = jnp.concatenate([pieces] * experts, axis=0).astype(BF)
    first = PIECES + 3 + SECTIONS
    copies += [
        pltpu.make_async_copy(stage_ref.at[:, BLOCK_WIDTH:], out_hbm.at[:, BLOCK_WIDTH:], sems.at[first]),
        pltpu.make_async_copy(scores_ref, scores_hbm, sems.at[first + 1]),
    ]
    for copy in copies[-2:]:
        copy.start()
    for copy in copies:
        copy.wait()


def weights_kernel(
    block_ref,
    owner_ref,
    top_ref,
    rest_ref,
    positives_ref,
    scores_hbm,
    query_hbm,
    _left_hbm,
    _right_hbm,
    out_ref,
    pieces_ref,
    code_weights_ref,
    scores_ref,
    query_ref,
    sems,
):
    copies = [
        pltpu.make_async_copy(scores_hbm, scores_ref, sems.at[0]),
        pltpu.make_async_copy(query_hbm, query_ref, sems.at[1]),
    ]
    for copy in copies:
        copy.start()
    pieces_ref[...] = block_ref[:, BLOCK_WIDTH:].astype(F32)
    peers, columns = block_ref.shape[0] // BLOCK, scores_ref.shape[0]
    owner = owner_ref[0]
    own = iota((peers, 1), 0) == owner
    column = owner * columns + iota((columns, 1), 0)
    copies[0].wait()
    for c in range(PIECES):
        lanes = slice(c * LANES, (c + 1) * LANES)
        sums = (
            pieces_ref[pl.ds(c, peers, stride=BLOCK), :]
            + pieces_ref[pl.ds(PIECES + c, peers, stride=BLOCK), :]
        )
        row_top = jnp.max(sums, axis=0, keepdims=True)
        shares = jnp.exp(sums - row_top)
        total = jnp.sum(shares, axis=0, keepdims=True)
        rest = jnp.sum(jnp.where(own, 0.0, shares), axis=0, keepdims=True)
        rest = rest + rest_ref[:, lanes] * jnp.exp(top_ref[:, lanes] - row_top)
        part = jnp.where(positives_ref[:, lanes] == column, -rest, jnp.exp(scores_ref[:, lanes] - row_top))
        code_weights_ref[:, lanes] = (part * (GRAD_SCALE / total)).astype(BF)
    copies[1].wait()
    out_ref[...] = dot(code_weights_ref[...], query_ref[...]).astype(BF)


def cotangent_kernel(parts_ref, lengths_ref, q_ref, out_hbm, token_hbm, token_ref, stage_ref, sems):
    files, tokens = lengths_ref.shape[1], token_ref.shape[0]
    row, position = iota((files, 1), 0), iota((1, tokens), 1)
    length = jnp.zeros((files, 1), jnp.int32)
    segment = jnp.zeros((1, tokens), jnp.int32)
    end = jnp.int32(0)
    for f in range(files):
        length = jnp.where(row == f, lengths_ref[0, f], length)
        end = end + lengths_ref[0, f]
        segment = segment + (position >= end).astype(jnp.int32)
    code_grad = parts_ref[0:files, :].astype(F32)
    for part in range(1, parts_ref.shape[0] // files):
        code_grad = code_grad + parts_ref[part * files : (part + 1) * files, :].astype(F32)
    file_cot = (code_grad / length.astype(F32)).astype(BF)
    member = (iota((files, tokens), 0) == segment).astype(F32).astype(BF)
    token_ref[...] = dot_first(member, file_cot).astype(BF)
    keep = pltpu.make_async_copy(token_ref, token_hbm, sems.at[SECTIONS])
    keep.start()
    for copy in pack_rows(token_ref, q_ref[...], stage_ref, out_hbm, sems.at[0:SECTIONS]):
        copy.wait()
    keep.wait()


def halves(total):
    return 2 if total % 512 == 0 else 1


def unpack_blocks(block_ref, rows_ref):
    parts = halves(block_ref.shape[0])
    height = block_ref.shape[0] // parts
    wide = height // BLOCK * SLOTS
    i, r = iota((wide, height), 0), iota((wide, height), 1)
    peer, j = r >> 3, r & (BLOCK - 1)
    main = ((i == peer * SLOTS + j) & (j < SLOTS)).astype(F32).astype(BF)
    for g in range(parts):
        rows = slice(g * wide, (g + 1) * wide)
        tail = jnp.zeros((wide, SECTION), F32)
        for k in range(SECTIONS):
            last = ((i == peer * SLOTS + (j - SLOTS) * 3 + k) & (j >= SLOTS)).astype(F32).astype(BF)
            both = dot(
                jnp.concatenate([main, last], axis=0),
                block_ref[g * height : (g + 1) * height, section(k)],
            )
            rows_ref[rows, section(k)] = both[:wide].astype(BF)
            tail = tail + both[wide:]
        rows_ref[rows, section(SECTIONS)] = tail.astype(BF)


def pack_blocks(rows_ref, block_ref):
    parts = halves(block_ref.shape[0])
    height = block_ref.shape[0] // parts
    wide = height // BLOCK * SLOTS
    r, i = iota((height, wide), 0), iota((height, wide), 1)
    peer, j = r >> 3, r & (BLOCK - 1)
    main = ((i == peer * SLOTS + j) & (j < SLOTS)).astype(F32).astype(BF)
    for g in range(parts):
        rows = slice(g * wide, (g + 1) * wide)
        tail = rows_ref[rows, section(SECTIONS)]
        for k in range(SECTIONS):
            last = ((i == peer * SLOTS + (j - SLOTS) * 3 + k) & (j >= SLOTS)).astype(F32).astype(BF)
            block_ref[g * height : (g + 1) * height, section(k)] = (
                dot(main, rows_ref[rows, section(k)]) + dot(last, tail)
            ).astype(BF)


def place_weights(shards, order_ref, weights_ref, columns, sems, first):
    copies = []
    for n, shard in enumerate(shards):
        rows = pl.ds(pl.multiple_of(order_ref[n], LANES), shard.shape[0])
        copies.append(
            pltpu.make_async_copy(
                shard.at[:, columns], weights_ref.at[rows, columns], sems.at[first + n]
            )
        )
    return copies


def forward_kernel(order_ref, block_ref, *refs):
    *shards, factor_ref, weights_ref, rows_ref, sems = refs
    hidden = factor_ref.shape[1] // 2
    copies = place_weights(shards, order_ref, weights_ref, slice(0, 2 * hidden), sems, 0)
    for copy in copies:
        copy.start()
    unpack_blocks(block_ref, rows_ref)
    for copy in copies:
        copy.wait()
    gate_pre = dot(rows_ref[...], weights_ref[:, :hidden])
    up_pre = dot(rows_ref[...], weights_ref[:, hidden:])
    s = jax.nn.sigmoid(gate_pre)
    factor_ref[:, :hidden] = up_pre * s * (1.0 + gate_pre * (1.0 - s))
    factor_ref[:, hidden:] = gate_pre * s


def backward_kernel(order_ref, block_hbm, factor_hbm, *refs):
    *shards, out_ref, block_ref, weights_ref, factor_ref, rows_ref, hidden_ref, sems = refs
    hidden = factor_ref.shape[1] // 2
    parts = halves(block_ref.shape[0])
    height = block_ref.shape[0] // parts
    first = [
        pltpu.make_async_copy(
            block_hbm.at[g * height : (g + 1) * height], block_ref.at[g * height : (g + 1) * height], sems.at[g]
        )
        for g in range(parts)
    ]
    down = place_weights(shards, order_ref, weights_ref, slice(2 * hidden, 3 * hidden), sems, parts)
    factor = pltpu.make_async_copy(factor_hbm, factor_ref, sems.at[parts + len(shards)])
    rest = place_weights(
        shards, order_ref, weights_ref, slice(0, 2 * hidden), sems, parts + len(shards) + 1
    )
    for copy in (*first, *down, factor, *rest):
        copy.start()
    for copy in first:
        copy.wait()
    unpack_blocks(block_ref, rows_ref)
    for copy in down:
        copy.wait()
    back = dot(rows_ref[...], weights_ref[:, 2 * hidden :])
    factor.wait()
    hidden_ref[:, :hidden] = (back * factor_ref[:, :hidden]).astype(BF)
    hidden_ref[:, hidden:] = (back * factor_ref[:, hidden:]).astype(BF)
    for copy in rest:
        copy.wait()
    for k in range(SECTIONS + 1):
        rows_ref[:, section(k)] = dot_last(
            hidden_ref[...], weights_ref[section(k), : 2 * hidden]
        ).astype(BF)
    pack_blocks(rows_ref, out_ref)


def finish_kernel(
    block_ref, residual_ref, gain_ref, q_ref, units_ref, token_ref, out_ref, grad_ref
):
    total, q = block_ref.shape[0], q_ref[...]
    gates = units_ref[...].astype(F32) * (1.0 / 256.0)
    first, second = gates[0:1], gates[1:2]
    tokens = q.shape[1]
    main = picks(total, q, first, second)
    tail = jnp.zeros((tokens, SECTION), F32)
    for k in range(SECTIONS):
        both = dot_first(
            jnp.concatenate([main, picks(total, tail_row(q, k), first, second)], axis=1),
            block_ref[:, section(k)],
        )
        grad_ref[:, section(k)] = both[:tokens]
        tail = tail + both[tokens:]
    grad_ref[:, section(SECTIONS)] = tail
    stream = residual_ref[...].astype(F32)
    root = inverse_rms(stream)
    scaled = gain_ref[...].astype(F32) * grad_ref[...]
    correction = jnp.mean(scaled * stream, axis=-1, keepdims=True)
    cot = token_ref[...].astype(F32)
    out_ref[...] = (cot + root * scaled - stream * (root * root * root * correction)).astype(BF)


def params(mib):
    return pltpu.CompilerParams(vmem_limit_bytes=mib << 20)


IN_SMEM = pl.BlockSpec(memory_space=pltpu.SMEM)
IN_VMEM = pl.BlockSpec(memory_space=pltpu.VMEM)
IN_HBM = pl.BlockSpec(memory_space=pltpu.HBM)


def hbm(value):
    return pltpu.with_memory_space_constraint(value, pltpu.HBM)


def per_device(
    query_reps,
    code_reps,
    positives,
    file_lengths,
    residual,
    norm_gain,
    expert_ids,
    gate_units,
    w_gate,
    w_up,
    w_down,
):
    owners = lax.axis_size("expert")
    columns = code_reps.shape[0]
    queries, width = query_reps.shape
    files = file_lengths.shape[2]
    tokens = residual.shape[1]
    hidden = w_gate.shape[2]
    total = owners * BLOCK
    lengths = file_lengths.reshape(1, files)
    stream = residual[0]
    gain = norm_gain.reshape(1, width)
    ids = expert_ids[0].T
    units = gate_units[0].T

    owner = lax.axis_index("expert")[None]

    def exchange(value):
        shape = value.shape
        return lax.all_to_all(
            value.reshape(owners, BLOCK, shape[1]), "expert", 0, 0, tiled=True
        ).reshape(shape)

    blocks, scores, q, local_top, local_rest, joined = pl.pallas_call(
        functools.partial(dispatch_kernel, experts=owners),
        out_shape=(
            pltpu.HBM((total, BLOCK_WIDTH + LANES), BF),
            pltpu.HBM((columns, queries), F32),
            jax.ShapeDtypeStruct((2, tokens), jnp.int32),
            jax.ShapeDtypeStruct((1, queries), F32),
            jax.ShapeDtypeStruct((1, queries), F32),
            jax.ShapeDtypeStruct((w_gate.shape[1], 3 * hidden), BF),
        ),
        in_specs=[IN_SMEM] + [IN_VMEM] * 5 + [IN_HBM] * 4,
        out_specs=(IN_HBM, IN_HBM) + (IN_VMEM,) * 4,
        scratch_shapes=[
            pltpu.VMEM((queries, width), BF),
            pltpu.VMEM((columns, queries), F32),
            pltpu.VMEM((tokens, width), BF),
            pltpu.VMEM((total, BLOCK_WIDTH + LANES), BF),
            pltpu.SemaphoreType.DMA((PIECES + 5 + SECTIONS,)),
        ],
        compiler_params=params(16),
        name="dispatch",
    )(
        owner,
        stream,
        gain,
        ids,
        code_reps,
        positives[None],
        hbm(query_reps),
        hbm(w_gate[0]),
        hbm(w_up[0]),
        hbm(w_down[0]),
    )
    size = lax.axis_size("dp")
    me = lax.axis_index("dp")
    half = joined.shape[0] // 2

    def ahead(value, step):
        return lax.ppermute(value, "dp", [(d, (d + step) % size) for d in range(size)])

    def partner(value):
        return lax.ppermute(value, "dp", [(d, d ^ 1) for d in range(size)])

    from_left, from_right = ahead(joined, 2), ahead(joined, size - 2)
    blocks = exchange(blocks)
    parts = pl.pallas_call(
        weights_kernel,
        out_shape=jax.ShapeDtypeStruct((columns, width), BF),
        in_specs=[IN_VMEM, IN_SMEM] + [IN_VMEM] * 3 + [IN_HBM] * 4,
        out_specs=IN_VMEM,
        scratch_shapes=[
            pltpu.VMEM((total, LANES), F32),
            pltpu.VMEM((columns, queries), BF),
            pltpu.VMEM((columns, queries), F32),
            pltpu.VMEM((queries, width), BF),
            pltpu.SemaphoreType.DMA((2,)),
        ],
        compiler_params=params(12),
        name="code_weights",
    )(
        blocks,
        owner,
        local_top,
        local_rest,
        positives[None],
        hbm(scores),
        hbm(query_reps),
        hbm(from_left),
        hbm(from_right),
    )
    parts = lax.all_to_all(
        parts.reshape(columns // files, files, width), "dp", 0, 0, tiled=True
    ).reshape(columns, width)
    cot_blocks, token_cot = pl.pallas_call(
        cotangent_kernel,
        out_shape=(
            pltpu.HBM((total, BLOCK_WIDTH), BF),
            pltpu.HBM((tokens, width), BF),
        ),
        in_specs=[IN_VMEM, IN_SMEM, IN_VMEM],
        out_specs=(IN_HBM, IN_HBM),
        scratch_shapes=[
            pltpu.VMEM((tokens, width), BF),
            pltpu.VMEM((total, BLOCK_WIDTH), BF),
            pltpu.SemaphoreType.DMA((SECTIONS + 1,)),
        ],
        compiler_params=params(12),
        name="cotangent",
    )(parts, lengths, q)
    cot_blocks = exchange(cot_blocks)
    joined, from_left, from_right, _ = lax.optimization_barrier((joined, from_left, from_right, parts))
    shards = [
        joined,
        from_left,
        from_right,
        ahead(from_left[:half], 2),
        ahead(from_right[half:], size - 2),
    ]
    shards = [hbm(shard) for shard in shards + [partner(shard) for shard in shards]]
    height = joined.shape[0]
    order = jnp.stack(
        [
            jnp.bitwise_and(d + step, size - 1) * height + start
            for d in (me, me ^ 1)
            for step, start in ((0, 0), (size - 2, 0), (2, 0), (4, 0), (4, half))
        ]
    ).astype(jnp.int32)

    rows = owners * SLOTS
    factor = pl.pallas_call(
        forward_kernel,
        out_shape=jax.ShapeDtypeStruct((rows, 2 * hidden), F32),
        in_specs=[IN_SMEM, IN_VMEM] + [IN_HBM] * len(shards),
        out_specs=IN_VMEM,
        scratch_shapes=[
            pltpu.VMEM((width, 2 * hidden), BF),
            pltpu.VMEM((rows, width), BF),
            pltpu.SemaphoreType.DMA((len(shards),)),
        ],
        compiler_params=params(24),
        name="expert_forward",
    )(order, blocks, *shards)
    result = pl.pallas_call(
        backward_kernel,
        out_shape=jax.ShapeDtypeStruct((total, BLOCK_WIDTH), BF),
        in_specs=[IN_SMEM] + [IN_HBM] * (2 + len(shards)),
        out_specs=IN_VMEM,
        scratch_shapes=[
            pltpu.VMEM((total, BLOCK_WIDTH), BF),
            pltpu.VMEM((width, 3 * hidden), BF),
            pltpu.VMEM((rows, 2 * hidden), F32),
            pltpu.VMEM((rows, width), BF),
            pltpu.VMEM((rows, 2 * hidden), BF),
            pltpu.SemaphoreType.DMA((halves(total) + 2 * len(shards) + 1,)),
        ],
        compiler_params=params(32),
        name="expert_backward",
    )(order, hbm(cot_blocks), hbm(factor), *shards)

    token_grad = pl.pallas_call(
        finish_kernel,
        out_shape=jax.ShapeDtypeStruct((tokens, width), BF),
        in_specs=[IN_VMEM] * 6,
        out_specs=IN_VMEM,
        scratch_shapes=[pltpu.VMEM((tokens, width), F32)],
        compiler_params=params(12),
        name="finish",
    )(exchange(result), stream, gain, q, units, token_cot)
    return token_grad[None]


def solution(mesh):
    return jax.shard_map(
        per_device,
        mesh=mesh,
        in_specs=(
            P("dp", None),
            P("expert", None),
            P("dp"),
            P("expert", "dp", None),
            P("expert", "dp", None),
            P(),
            P("expert", "dp", None),
            P("expert", "dp", None),
            P("expert", "dp", None),
            P("expert", "dp", None),
            P("expert", "dp", None),
        ),
        out_specs=P("expert", "dp", None),
        check_vma=False,
    )
```

```python
import functools
import jax
import jax.numpy as jnp
from jax import lax
from jax.experimental import pallas as pl
from jax.experimental.pallas import tpu as pltpu
from jax.sharding import PartitionSpec as P

SCORE_SCALE = 20.0
GRAD_SCALE = 2560.0
EPSILON = 1e-06
BF = jnp.bfloat16
F32 = jnp.float32

SLOTS = 6
BLOCK = 8
SECTION = 512
SECTIONS = 3
BLOCK_WIDTH = SECTIONS * SECTION
LANES = 128
PIECES = 4


def iota(shape, dim):
    return lax.broadcasted_iota(jnp.int32, shape, dim)


def dot(a, b):
    return jnp.dot(a, b, preferred_element_type=F32)


def dot_first(a, b):
    return lax.dot_general(a, b, (((0,), (0,)), ((), ())), preferred_element_type=F32)


def dot_last(a, b):
    return lax.dot_general(a, b, (((1,), (1,)), ((), ())), preferred_element_type=F32)


def section(k):
    return slice(k * SECTION, (k + 1) * SECTION)


def tail_row(q, k):
    rank = jnp.bitwise_and(q, BLOCK - 1)
    high = (rank >= 3).astype(jnp.int32)
    return jnp.where(rank - 3 * high == k, q - rank + SLOTS + high, -1)


def picks(rows, q, first, second):
    r = iota((rows, q.shape[1]), 0)
    zero = jnp.zeros((), F32)
    return (jnp.where(r == q[0:1], first, zero) + jnp.where(r == q[1:2], second, zero)).astype(BF)


def pack_rows(rows_ref, q, stage_ref, out_hbm, sems):
    total = stage_ref.shape[0]
    main = picks(total, q, 1.0, 1.0)
    tail = rows_ref[:, section(SECTIONS)]
    copies = []
    for k in range(SECTIONS):
        left = jnp.concatenate([main, picks(total, tail_row(q, k), 1.0, 1.0)], axis=1)
        right = jnp.concatenate([rows_ref[:, section(k)], tail], axis=0)
        stage_ref[:, section(k)] = dot(left, right).astype(BF)
        copies.append(
            pltpu.make_async_copy(stage_ref.at[:, section(k)], out_hbm.at[:, section(k)], sems.at[k])
        )
        copies[-1].start()
    return copies


def inverse_rms(stream):
    return lax.rsqrt(jnp.mean(stream * stream, axis=-1, keepdims=True) + EPSILON)


def dispatch_kernel(
    owner_ref,
    ids_hbm,
    residual_hbm,
    gain_hbm,
    code_hbm,
    positives_hbm,
    query_hbm,
    w0_hbm,
    w1_hbm,
    w2_hbm,
    out_hbm,
    scores_hbm,
    q_ref,
    top_ref,
    rest_ref,
    joined_ref,
    ids_ref,
    residual_ref,
    gain_ref,
    code_ref,
    positives_ref,
    query_ref,
    scores_ref,
    normed_ref,
    stage_ref,
    sems,
    *,
    experts,
):
    hidden, columns = w0_hbm.shape[1], code_ref.shape[0]
    base = PIECES + 5 + SECTIONS
    inputs = [
        pltpu.make_async_copy(source, target, sems.at[base + n])
        for n, (source, target) in enumerate(
            (
                (ids_hbm, ids_ref),
                (residual_hbm, residual_ref),
                (gain_hbm, gain_ref),
                (code_hbm, code_ref),
                (positives_hbm, positives_ref),
            )
        )
    ]
    for copy in inputs:
        copy.start()
    parts = [slice(c * LANES, (c + 1) * LANES) for c in range(PIECES)]
    queries = [
        pltpu.make_async_copy(query_hbm.at[part], query_ref.at[part], sems.at[c])
        for c, part in enumerate(parts)
    ]
    for copy in queries:
        copy.start()
    copies = [
        pltpu.make_async_copy(w_hbm, joined_ref.at[:, k * hidden : (k + 1) * hidden], sems.at[PIECES + k])
        for k, w_hbm in enumerate((w0_hbm, w1_hbm, w2_hbm))
    ]
    for copy in copies:
        copy.start()
    for copy in inputs:
        copy.wait()
    stream = residual_ref[...].astype(F32)
    scaled = stream * inverse_rms(stream)
    gain = gain_ref[...].astype(F32)
    for c in range(gain.shape[0]):
        lanes = slice(c * LANES, (c + 1) * LANES)
        normed_ref[:, lanes] = (scaled[:, lanes] * gain[c : c + 1]).astype(BF)
    ids = jnp.concatenate([ids_ref[0:1, :], ids_ref[1:2, :]], axis=1)
    count = ids.shape[1]
    table = (iota((experts, count), 0) == ids).astype(F32)
    earlier = dot(
        table.astype(BF), (iota((count, count), 0) < iota((count, count), 1)).astype(F32).astype(BF)
    )
    rank = jnp.sum(table * earlier, axis=0, keepdims=True).astype(jnp.int32)
    q_flat = ids * BLOCK + rank
    half = count // 2
    q = jnp.concatenate([q_flat[:, :half], q_flat[:, half:]], axis=0)
    q_ref[...] = q
    copies += pack_rows(normed_ref, q, stage_ref, out_hbm, sems.at[PIECES + 3 : PIECES + 3 + SECTIONS])
    column = owner_ref[0] * columns + iota((columns, 1), 0)
    high, low = [], []
    for copy, part in zip(queries, parts):
        copy.wait()
        scores = dot_last(code_ref[...], query_ref[part, :]) * SCORE_SCALE
        scores_ref[:, part] = scores
        top = jnp.max(scores, axis=0, keepdims=True)
        exponent = jnp.exp(scores - top)
        top_ref[:, part] = top
        rest_ref[:, part] = jnp.sum(
            jnp.where(positives_ref[:, part] == column, 0.0, exponent), axis=0, keepdims=True
        )
        log_sum = top + jnp.log(jnp.sum(exponent, axis=0, keepdims=True))
        high.append(log_sum.astype(BF).astype(F32))
        low.append(log_sum - high[-1])
    pieces = jnp.concatenate(high + low, axis=0)
    stage_ref[:, BLOCK_WIDTH:] = jnp.concatenate([pieces] * experts, axis=0).astype(BF)
    first = PIECES + 3 + SECTIONS
    copies += [
        pltpu.make_async_copy(stage_ref.at[:, BLOCK_WIDTH:], out_hbm.at[:, BLOCK_WIDTH:], sems.at[first]),
        pltpu.make_async_copy(scores_ref, scores_hbm, sems.at[first + 1]),
    ]
    for copy in copies[-2:]:
        copy.start()
    for copy in copies:
        copy.wait()


def weights_kernel(
    block_ref,
    owner_ref,
    top_ref,
    rest_ref,
    positives_ref,
    scores_hbm,
    query_hbm,
    _left_hbm,
    _right_hbm,
    out_ref,
    pieces_ref,
    code_weights_ref,
    scores_ref,
    query_ref,
    sems,
):
    copies = [
        pltpu.make_async_copy(scores_hbm, scores_ref, sems.at[0]),
        pltpu.make_async_copy(query_hbm, query_ref, sems.at[1]),
    ]
    for copy in copies:
        copy.start()
    pieces_ref[...] = block_ref[:, BLOCK_WIDTH:].astype(F32)
    peers, columns = block_ref.shape[0] // BLOCK, scores_ref.shape[0]
    owner = owner_ref[0]
    own = iota((peers, 1), 0) == owner
    column = owner * columns + iota((columns, 1), 0)
    copies[0].wait()
    for c in range(PIECES):
        lanes = slice(c * LANES, (c + 1) * LANES)
        sums = (
            pieces_ref[pl.ds(c, peers, stride=BLOCK), :]
            + pieces_ref[pl.ds(PIECES + c, peers, stride=BLOCK), :]
        )
        row_top = jnp.max(sums, axis=0, keepdims=True)
        shares = jnp.exp(sums - row_top)
        total = jnp.sum(shares, axis=0, keepdims=True)
        rest = jnp.sum(jnp.where(own, 0.0, shares), axis=0, keepdims=True)
        rest = rest + rest_ref[:, lanes] * jnp.exp(top_ref[:, lanes] - row_top)
        part = jnp.where(positives_ref[:, lanes] == column, -rest, jnp.exp(scores_ref[:, lanes] - row_top))
        code_weights_ref[:, lanes] = (part * (GRAD_SCALE / total)).astype(BF)
    copies[1].wait()
    out_ref[...] = dot(code_weights_ref[...], query_ref[...]).astype(BF)


def cotangent_kernel(parts_ref, lengths_ref, q_ref, out_hbm, token_hbm, token_ref, stage_ref, sems):
    files, tokens = lengths_ref.shape[1], token_ref.shape[0]
    row, position = iota((files, 1), 0), iota((1, tokens), 1)
    length = jnp.zeros((files, 1), jnp.int32)
    segment = jnp.zeros((1, tokens), jnp.int32)
    end = jnp.int32(0)
    for f in range(files):
        length = jnp.where(row == f, lengths_ref[0, f], length)
        end = end + lengths_ref[0, f]
        segment = segment + (position >= end).astype(jnp.int32)
    code_grad = parts_ref[0:files, :].astype(F32)
    for part in range(1, parts_ref.shape[0] // files):
        code_grad = code_grad + parts_ref[part * files : (part + 1) * files, :].astype(F32)
    file_cot = (code_grad / length.astype(F32)).astype(BF)
    member = (iota((files, tokens), 0) == segment).astype(F32).astype(BF)
    token_ref[...] = dot_first(member, file_cot).astype(BF)
    keep = pltpu.make_async_copy(token_ref, token_hbm, sems.at[SECTIONS])
    keep.start()
    for copy in pack_rows(token_ref, q_ref[...], stage_ref, out_hbm, sems.at[0:SECTIONS]):
        copy.wait()
    keep.wait()


def halves(total):
    return 2 if total % 512 == 0 else 1


def unpack_blocks(block_ref, rows_ref):
    parts = halves(block_ref.shape[0])
    height = block_ref.shape[0] // parts
    wide = height // BLOCK * SLOTS
    i, r = iota((wide, height), 0), iota((wide, height), 1)
    peer, j = r >> 3, r & (BLOCK - 1)
    main = ((i == peer * SLOTS + j) & (j < SLOTS)).astype(F32).astype(BF)
    for g in range(parts):
        rows = slice(g * wide, (g + 1) * wide)
        tail = jnp.zeros((wide, SECTION), F32)
        for k in range(SECTIONS):
            last = ((i == peer * SLOTS + (j - SLOTS) * 3 + k) & (j >= SLOTS)).astype(F32).astype(BF)
            both = dot(
                jnp.concatenate([main, last], axis=0),
                block_ref[g * height : (g + 1) * height, section(k)],
            )
            rows_ref[rows, section(k)] = both[:wide].astype(BF)
            tail = tail + both[wide:]
        rows_ref[rows, section(SECTIONS)] = tail.astype(BF)


def pack_blocks(rows_ref, block_ref):
    parts = halves(block_ref.shape[0])
    height = block_ref.shape[0] // parts
    wide = height // BLOCK * SLOTS
    r, i = iota((height, wide), 0), iota((height, wide), 1)
    peer, j = r >> 3, r & (BLOCK - 1)
    main = ((i == peer * SLOTS + j) & (j < SLOTS)).astype(F32).astype(BF)
    for g in range(parts):
        rows = slice(g * wide, (g + 1) * wide)
        tail = rows_ref[rows, section(SECTIONS)]
        for k in range(SECTIONS):
            last = ((i == peer * SLOTS + (j - SLOTS) * 3 + k) & (j >= SLOTS)).astype(F32).astype(BF)
            block_ref[g * height : (g + 1) * height, section(k)] = (
                dot(main, rows_ref[rows, section(k)]) + dot(last, tail)
            ).astype(BF)


def forward_kernel(order_ref, block_ref, *refs):
    *shards, weights_hbm, factor_hbm, weights_ref, factor_ref, rows_ref, sems = refs
    hidden = factor_ref.shape[1] // 2
    copies = []
    for n, shard in enumerate(shards):
        rows = pl.ds(pl.multiple_of(order_ref[n], LANES), shard.shape[0])
        copies.append(pltpu.make_async_copy(shard, weights_ref.at[rows], sems.at[n]))
    for copy in copies:
        copy.start()
    unpack_blocks(block_ref, rows_ref)
    for copy in copies:
        copy.wait()
    keep = [
        pltpu.make_async_copy(weights_ref, weights_hbm, sems.at[len(shards)]),
        pltpu.make_async_copy(factor_ref, factor_hbm, sems.at[len(shards) + 1]),
    ]
    keep[0].start()
    gate_pre = dot(rows_ref[...], weights_ref[:, :hidden])
    up_pre = dot(rows_ref[...], weights_ref[:, hidden : 2 * hidden])
    s = jax.nn.sigmoid(gate_pre)
    factor_ref[:, :hidden] = up_pre * s * (1.0 + gate_pre * (1.0 - s))
    factor_ref[:, hidden:] = gate_pre * s
    keep[1].start()
    for copy in keep:
        copy.wait()


def backward_kernel(
    block_hbm, weights_hbm, factor_hbm, out_ref, block_ref, weights_ref, factor_ref, rows_ref, hidden_ref, sems
):
    hidden = factor_ref.shape[1] // 2
    down, rest = slice(2 * hidden, 3 * hidden), slice(0, 2 * hidden)
    copies = [
        pltpu.make_async_copy(source, target, sems.at[n])
        for n, (source, target) in enumerate(
            (
                (block_hbm, block_ref),
                (weights_hbm.at[:, down], weights_ref.at[:, down]),
                (factor_hbm, factor_ref),
                (weights_hbm.at[:, rest], weights_ref.at[:, rest]),
            )
        )
    ]
    for copy in copies:
        copy.start()
    copies[0].wait()
    unpack_blocks(block_ref, rows_ref)
    copies[1].wait()
    back = dot(rows_ref[...], weights_ref[:, down])
    copies[2].wait()
    hidden_ref[:, :hidden] = (back * factor_ref[:, :hidden]).astype(BF)
    hidden_ref[:, hidden:] = (back * factor_ref[:, hidden:]).astype(BF)
    copies[3].wait()
    for k in range(SECTIONS + 1):
        rows_ref[:, section(k)] = dot_last(hidden_ref[...], weights_ref[section(k), rest]).astype(BF)
    pack_blocks(rows_ref, out_ref)


def finish_kernel(
    block_ref, residual_ref, gain_ref, q_ref, units_ref, token_ref, out_ref, grad_ref
):
    total, q = block_ref.shape[0], q_ref[...]
    gates = units_ref[...].astype(F32) * (1.0 / 256.0)
    first, second = gates[0:1], gates[1:2]
    tokens = q.shape[1]
    main = picks(total, q, first, second)
    tail = jnp.zeros((tokens, SECTION), F32)
    for k in range(SECTIONS):
        both = dot_first(
            jnp.concatenate([main, picks(total, tail_row(q, k), first, second)], axis=1),
            block_ref[:, section(k)],
        )
        grad_ref[:, section(k)] = both[:tokens]
        tail = tail + both[tokens:]
    grad_ref[:, section(SECTIONS)] = tail
    stream = residual_ref[...].astype(F32)
    root = inverse_rms(stream)
    gain = gain_ref[...].astype(F32)
    for c in range(gain.shape[0]):
        lanes = slice(c * LANES, (c + 1) * LANES)
        grad_ref[:, lanes] = gain[c : c + 1] * grad_ref[:, lanes]
    scaled = grad_ref[...]
    correction = jnp.mean(scaled * stream, axis=-1, keepdims=True)
    cot = token_ref[...].astype(F32)
    out_ref[...] = (cot + root * scaled - stream * (root * root * root * correction)).astype(BF)


def params(mib):
    return pltpu.CompilerParams(vmem_limit_bytes=mib << 20)


IN_SMEM = pl.BlockSpec(memory_space=pltpu.SMEM)
IN_VMEM = pl.BlockSpec(memory_space=pltpu.VMEM)
IN_HBM = pl.BlockSpec(memory_space=pltpu.HBM)


def hbm(value):
    return pltpu.with_memory_space_constraint(value, pltpu.HBM)


def per_device(
    query_reps,
    code_reps,
    positives,
    file_lengths,
    residual,
    norm_gain,
    expert_ids,
    gate_units,
    w_gate,
    w_up,
    w_down,
):
    owners = lax.axis_size("expert")
    columns = code_reps.shape[0]
    queries, width = query_reps.shape
    files = file_lengths.shape[2]
    tokens = residual.shape[1]
    hidden = w_gate.shape[2]
    total = owners * BLOCK
    lengths = file_lengths.reshape(1, files)
    stream = residual[0]
    gain = norm_gain.reshape(width // LANES, LANES)
    ids = expert_ids[0].T
    units = gate_units[0].T

    owner = lax.axis_index("expert")[None]

    def exchange(value):
        shape = value.shape
        return lax.all_to_all(
            value.reshape(owners, BLOCK, shape[1]), "expert", 0, 0, tiled=True
        ).reshape(shape)

    blocks, scores, q, local_top, local_rest, joined = pl.pallas_call(
        functools.partial(dispatch_kernel, experts=owners),
        out_shape=(
            pltpu.HBM((total, BLOCK_WIDTH + LANES), BF),
            pltpu.HBM((columns, queries), F32),
            jax.ShapeDtypeStruct((2, tokens), jnp.int32),
            jax.ShapeDtypeStruct((1, queries), F32),
            jax.ShapeDtypeStruct((1, queries), F32),
            jax.ShapeDtypeStruct((w_gate.shape[1], 3 * hidden), BF),
        ),
        in_specs=[IN_SMEM] + [IN_HBM] * 9,
        out_specs=(IN_HBM, IN_HBM) + (IN_VMEM,) * 4,
        scratch_shapes=[
            pltpu.VMEM((2, tokens), jnp.int32),
            pltpu.VMEM((tokens, width), BF),
            pltpu.VMEM(gain.shape, BF),
            pltpu.VMEM((columns, width), BF),
            pltpu.VMEM((1, queries), jnp.int32),
            pltpu.VMEM((queries, width), BF),
            pltpu.VMEM((columns, queries), F32),
            pltpu.VMEM((tokens, width), BF),
            pltpu.VMEM((total, BLOCK_WIDTH + LANES), BF),
            pltpu.SemaphoreType.DMA((PIECES + 10 + SECTIONS,)),
        ],
        compiler_params=params(16),
        name="dispatch",
    )(
        owner,
        hbm(ids),
        hbm(stream),
        hbm(gain),
        hbm(code_reps),
        hbm(positives[None]),
        hbm(query_reps),
        hbm(w_gate[0]),
        hbm(w_up[0]),
        hbm(w_down[0]),
    )
    size = lax.axis_size("dp")
    me = lax.axis_index("dp")
    half = joined.shape[0] // 2

    def ahead(value, step):
        return lax.ppermute(value, "dp", [(d, (d + step) % size) for d in range(size)])

    def partner(value):
        return lax.ppermute(value, "dp", [(d, d ^ 1) for d in range(size)])

    from_left, from_right = ahead(joined, 2), ahead(joined, size - 2)
    blocks = exchange(blocks)
    parts = pl.pallas_call(
        weights_kernel,
        out_shape=jax.ShapeDtypeStruct((columns, width), BF),
        in_specs=[IN_VMEM, IN_SMEM] + [IN_VMEM] * 3 + [IN_HBM] * 4,
        out_specs=IN_VMEM,
        scratch_shapes=[
            pltpu.VMEM((total, LANES), F32),
            pltpu.VMEM((columns, queries), BF),
            pltpu.VMEM((columns, queries), F32),
            pltpu.VMEM((queries, width), BF),
            pltpu.SemaphoreType.DMA((2,)),
        ],
        compiler_params=params(12),
        name="code_weights",
    )(
        blocks,
        owner,
        local_top,
        local_rest,
        positives[None],
        hbm(scores),
        hbm(query_reps),
        hbm(from_left),
        hbm(from_right),
    )
    parts = lax.all_to_all(
        parts.reshape(columns // files, files, width), "dp", 0, 0, tiled=True
    ).reshape(columns, width)
    cot_blocks, token_cot = pl.pallas_call(
        cotangent_kernel,
        out_shape=(
            pltpu.HBM((total, BLOCK_WIDTH), BF),
            pltpu.HBM((tokens, width), BF),
        ),
        in_specs=[IN_VMEM, IN_SMEM, IN_VMEM],
        out_specs=(IN_HBM, IN_HBM),
        scratch_shapes=[
            pltpu.VMEM((tokens, width), BF),
            pltpu.VMEM((total, BLOCK_WIDTH), BF),
            pltpu.SemaphoreType.DMA((SECTIONS + 1,)),
        ],
        compiler_params=params(12),
        name="cotangent",
    )(parts, lengths, q)
    cot_blocks = exchange(cot_blocks)
    joined, from_left, from_right, _ = lax.optimization_barrier((joined, from_left, from_right, parts))
    shards = [
        joined,
        from_left,
        from_right,
        ahead(from_left[:half], 2),
        ahead(from_right[half:], size - 2),
    ]
    shards = [hbm(shard) for shard in shards + [partner(shard) for shard in shards]]
    height = joined.shape[0]
    order = jnp.stack(
        [
            jnp.bitwise_and(d + step, size - 1) * height + start
            for d in (me, me ^ 1)
            for step, start in ((0, 0), (size - 2, 0), (2, 0), (4, 0), (4, half))
        ]
    ).astype(jnp.int32)

    rows = owners * SLOTS
    weights, factor = pl.pallas_call(
        forward_kernel,
        out_shape=(pltpu.HBM((width, 3 * hidden), BF), pltpu.HBM((rows, 2 * hidden), F32)),
        in_specs=[IN_SMEM, IN_VMEM] + [IN_HBM] * len(shards),
        out_specs=(IN_HBM, IN_HBM),
        scratch_shapes=[
            pltpu.VMEM((width, 3 * hidden), BF),
            pltpu.VMEM((rows, 2 * hidden), F32),
            pltpu.VMEM((rows, width), BF),
            pltpu.SemaphoreType.DMA((len(shards) + 2,)),
        ],
        compiler_params=params(32),
        name="expert_forward",
    )(order, blocks, *shards)
    result = pl.pallas_call(
        backward_kernel,
        out_shape=jax.ShapeDtypeStruct((total, BLOCK_WIDTH), BF),
        in_specs=[IN_HBM] * 3,
        out_specs=IN_VMEM,
        scratch_shapes=[
            pltpu.VMEM((total, BLOCK_WIDTH), BF),
            pltpu.VMEM((width, 3 * hidden), BF),
            pltpu.VMEM((rows, 2 * hidden), F32),
            pltpu.VMEM((rows, width), BF),
            pltpu.VMEM((rows, 2 * hidden), BF),
            pltpu.SemaphoreType.DMA((4,)),
        ],
        compiler_params=params(32),
        name="expert_backward",
    )(hbm(cot_blocks), hbm(weights), hbm(factor))

    token_grad = pl.pallas_call(
        finish_kernel,
        out_shape=jax.ShapeDtypeStruct((tokens, width), BF),
        in_specs=[IN_VMEM] * 6,
        out_specs=IN_VMEM,
        scratch_shapes=[pltpu.VMEM((tokens, width), F32)],
        compiler_params=params(12),
        name="finish",
    )(exchange(result), stream, gain, q, units, token_cot)
    return token_grad[None]


def solution(mesh):
    return jax.shard_map(
        per_device,
        mesh=mesh,
        in_specs=(
            P("dp", None),
            P("expert", None),
            P("dp"),
            P("expert", "dp", None),
            P("expert", "dp", None),
            P(),
            P("expert", "dp", None),
            P("expert", "dp", None),
            P("expert", "dp", None),
            P("expert", "dp", None),
            P("expert", "dp", None),
        ),
        out_specs=P("expert", "dp", None),
        check_vma=False,
    )
```

```python
import functools
import jax
import jax.numpy as jnp
from jax import lax
from jax.experimental import pallas as pl
from jax.experimental.pallas import tpu as pltpu
from jax.sharding import PartitionSpec as P

SCORE_SCALE = 20.0
GRAD_SCALE = 2560.0
EPSILON = 1e-06
BF = jnp.bfloat16
F32 = jnp.float32

SLOTS = 6
BLOCK = 8
SECTION = 512
SECTIONS = 3
BLOCK_WIDTH = SECTIONS * SECTION
LANES = 128
PIECES = 4


def iota(shape, dim):
    return lax.broadcasted_iota(jnp.int32, shape, dim)


def dot(a, b):
    return jnp.dot(a, b, preferred_element_type=F32)


def dot_first(a, b):
    return lax.dot_general(a, b, (((0,), (0,)), ((), ())), preferred_element_type=F32)


def dot_last(a, b):
    return lax.dot_general(a, b, (((1,), (1,)), ((), ())), preferred_element_type=F32)


def section(k):
    return slice(k * SECTION, (k + 1) * SECTION)


def tail_row(q, k):
    rank = jnp.bitwise_and(q, BLOCK - 1)
    high = (rank >= 3).astype(jnp.int32)
    return jnp.where(rank - 3 * high == k, q - rank + SLOTS + high, -1)


def picks(rows, q, first, second):
    r = iota((rows, q.shape[1]), 0)
    zero = jnp.zeros((), F32)
    return (jnp.where(r == q[0:1], first, zero) + jnp.where(r == q[1:2], second, zero)).astype(BF)


def pack_rows(rows_ref, q, stage_ref, out_hbm, sems):
    total = stage_ref.shape[0]
    main = picks(total, q, 1.0, 1.0)
    tail = rows_ref[:, section(SECTIONS)]
    copies = []
    for k in range(SECTIONS):
        left = jnp.concatenate([main, picks(total, tail_row(q, k), 1.0, 1.0)], axis=1)
        right = jnp.concatenate([rows_ref[:, section(k)], tail], axis=0)
        stage_ref[:, section(k)] = dot(left, right).astype(BF)
        copies.append(
            pltpu.make_async_copy(stage_ref.at[:, section(k)], out_hbm.at[:, section(k)], sems.at[k])
        )
        copies[-1].start()
    return copies


def inverse_rms(stream):
    return lax.rsqrt(jnp.mean(stream * stream, axis=-1, keepdims=True) + EPSILON)


def dispatch_kernel(
    owner_ref,
    ids_hbm,
    residual_hbm,
    gain_hbm,
    code_hbm,
    positives_hbm,
    query_hbm,
    w0_hbm,
    w1_hbm,
    w2_hbm,
    out_hbm,
    scores_hbm,
    q_ref,
    top_ref,
    rest_ref,
    joined_a_ref,
    joined_b_ref,
    ids_ref,
    residual_ref,
    gain_ref,
    code_ref,
    positives_ref,
    query_ref,
    scores_ref,
    normed_ref,
    stage_ref,
    sems,
    *,
    experts,
):
    hidden, columns = w0_hbm.shape[1], code_ref.shape[0]
    base = PIECES + 8 + SECTIONS
    inputs = [
        pltpu.make_async_copy(source, target, sems.at[base + n])
        for n, (source, target) in enumerate(
            (
                (ids_hbm, ids_ref),
                (residual_hbm, residual_ref),
                (gain_hbm, gain_ref),
                (code_hbm, code_ref),
                (positives_hbm, positives_ref),
            )
        )
    ]
    for copy in inputs:
        copy.start()
    parts = [slice(c * LANES, (c + 1) * LANES) for c in range(PIECES)]
    queries = [
        pltpu.make_async_copy(query_hbm.at[part], query_ref.at[part], sems.at[c])
        for c, part in enumerate(parts)
    ]
    for copy in queries:
        copy.start()
    half = joined_a_ref.shape[0]
    copies = [
        pltpu.make_async_copy(
            w_hbm.at[n * half : (n + 1) * half],
            joined_ref.at[:, k * hidden : (k + 1) * hidden],
            sems.at[PIECES + 2 * k + n],
        )
        for k, w_hbm in enumerate((w0_hbm, w1_hbm, w2_hbm))
        for n, joined_ref in enumerate((joined_a_ref, joined_b_ref))
    ]
    for copy in inputs:
        copy.wait()
    for copy in copies:
        copy.start()
    stream = residual_ref[...].astype(F32)
    scaled = stream * inverse_rms(stream)
    gain = gain_ref[...].astype(F32)
    for c in range(gain.shape[0]):
        lanes = slice(c * LANES, (c + 1) * LANES)
        normed_ref[:, lanes] = (scaled[:, lanes] * gain[c : c + 1]).astype(BF)
    ids = jnp.concatenate([ids_ref[0:1, :], ids_ref[1:2, :]], axis=1)
    count = ids.shape[1]
    table = (iota((experts, count), 0) == ids).astype(F32)
    earlier = dot(
        table.astype(BF), (iota((count, count), 0) < iota((count, count), 1)).astype(F32).astype(BF)
    )
    rank = jnp.sum(table * earlier, axis=0, keepdims=True).astype(jnp.int32)
    q_flat = ids * BLOCK + rank
    q = jnp.concatenate([q_flat[:, : count // 2], q_flat[:, count // 2 :]], axis=0)
    q_ref[...] = q
    copies += pack_rows(normed_ref, q, stage_ref, out_hbm, sems.at[PIECES + 6 : PIECES + 6 + SECTIONS])
    column = owner_ref[0] * columns + iota((columns, 1), 0)
    high, low = [], []
    for copy, part in zip(queries, parts):
        copy.wait()
        scores = dot_last(code_ref[...], query_ref[part, :]) * SCORE_SCALE
        scores_ref[:, part] = scores
        top = jnp.max(scores, axis=0, keepdims=True)
        exponent = jnp.exp(scores - top)
        top_ref[:, part] = top
        rest_ref[:, part] = jnp.sum(
            jnp.where(positives_ref[:, part] == column, 0.0, exponent), axis=0, keepdims=True
        )
        log_sum = top + jnp.log(jnp.sum(exponent, axis=0, keepdims=True))
        high.append(log_sum.astype(BF).astype(F32))
        low.append(log_sum - high[-1])
    pieces = jnp.concatenate(high + low, axis=0)
    stage_ref[:, BLOCK_WIDTH:] = jnp.concatenate([pieces] * experts, axis=0).astype(BF)
    first = PIECES + 6 + SECTIONS
    copies += [
        pltpu.make_async_copy(stage_ref.at[:, BLOCK_WIDTH:], out_hbm.at[:, BLOCK_WIDTH:], sems.at[first]),
        pltpu.make_async_copy(scores_ref, scores_hbm, sems.at[first + 1]),
    ]
    for copy in copies[-2:]:
        copy.start()
    for copy in copies:
        copy.wait()


def weights_kernel(
    block_ref,
    owner_ref,
    top_ref,
    rest_ref,
    positives_ref,
    scores_hbm,
    query_hbm,
    *refs,
):
    out_ref, pieces_ref, code_weights_ref, scores_ref, query_ref, sems = refs[-6:]
    copies = [pltpu.make_async_copy(scores_hbm, scores_ref, sems.at[PIECES])]
    copies += [
        pltpu.make_async_copy(
            query_hbm.at[c * LANES : (c + 1) * LANES], query_ref.at[c * LANES : (c + 1) * LANES], sems.at[c]
        )
        for c in range(PIECES)
    ]
    for copy in copies:
        copy.start()
    pieces_ref[...] = block_ref[:, BLOCK_WIDTH:].astype(F32)
    peers, columns = block_ref.shape[0] // BLOCK, scores_ref.shape[0]
    owner = owner_ref[0]
    own = iota((peers, 1), 0) == owner
    column = owner * columns + iota((columns, 1), 0)
    copies[0].wait()
    for c in range(PIECES):
        lanes = slice(c * LANES, (c + 1) * LANES)
        sums = (
            pieces_ref[pl.ds(c, peers, stride=BLOCK), :]
            + pieces_ref[pl.ds(PIECES + c, peers, stride=BLOCK), :]
        )
        row_top = jnp.max(sums, axis=0, keepdims=True)
        shares = jnp.exp(sums - row_top)
        total = jnp.sum(shares, axis=0, keepdims=True)
        rest = jnp.sum(jnp.where(own, 0.0, shares), axis=0, keepdims=True)
        rest = rest + rest_ref[:, lanes] * jnp.exp(top_ref[:, lanes] - row_top)
        part = jnp.where(positives_ref[:, lanes] == column, -rest, jnp.exp(scores_ref[:, lanes] - row_top))
        code_weights_ref[:, lanes] = (part * (GRAD_SCALE / total)).astype(BF)
    for copy in copies[1:]:
        copy.wait()
    out_ref[...] = dot(code_weights_ref[...], query_ref[...]).astype(BF)


def cotangent_kernel(parts_ref, lengths_ref, q_ref, out_hbm, token_hbm, token_ref, stage_ref, sems):
    files, tokens = lengths_ref.shape[1], token_ref.shape[0]
    row, position = iota((files, 1), 0), iota((1, tokens), 1)
    length = jnp.zeros((files, 1), jnp.int32)
    segment = jnp.zeros((1, tokens), jnp.int32)
    end = jnp.int32(0)
    for f in range(files):
        length = jnp.where(row == f, lengths_ref[0, f], length)
        end = end + lengths_ref[0, f]
        segment = segment + (position >= end).astype(jnp.int32)
    code_grad = parts_ref[0:files, :].astype(F32)
    for part in range(1, parts_ref.shape[0] // files):
        code_grad = code_grad + parts_ref[part * files : (part + 1) * files, :].astype(F32)
    file_cot = (code_grad / length.astype(F32)).astype(BF)
    member = (iota((files, tokens), 0) == segment).astype(F32).astype(BF)
    token_ref[...] = dot_first(member, file_cot).astype(BF)
    keep = pltpu.make_async_copy(token_ref, token_hbm, sems.at[SECTIONS])
    keep.start()
    for copy in pack_rows(token_ref, q_ref[...], stage_ref, out_hbm, sems.at[0:SECTIONS]):
        copy.wait()
    keep.wait()


def halves(total):
    return 2 if total % 512 == 0 else 1


def unpack_blocks(block_ref, rows_ref):
    parts = halves(block_ref.shape[0])
    height = block_ref.shape[0] // parts
    wide = height // BLOCK * SLOTS
    i, r = iota((wide, height), 0), iota((wide, height), 1)
    peer, j = r >> 3, r & (BLOCK - 1)
    main = ((i == peer * SLOTS + j) & (j < SLOTS)).astype(F32).astype(BF)
    for g in range(parts):
        rows = slice(g * wide, (g + 1) * wide)
        tail = jnp.zeros((wide, SECTION), F32)
        for k in range(SECTIONS):
            last = ((i == peer * SLOTS + (j - SLOTS) * 3 + k) & (j >= SLOTS)).astype(F32).astype(BF)
            both = dot(
                jnp.concatenate([main, last], axis=0),
                block_ref[g * height : (g + 1) * height, section(k)],
            )
            rows_ref[rows, section(k)] = both[:wide].astype(BF)
            tail = tail + both[wide:]
        rows_ref[rows, section(SECTIONS)] = tail.astype(BF)


def pack_blocks(rows_ref, block_ref):
    parts = halves(block_ref.shape[0])
    height = block_ref.shape[0] // parts
    wide = height // BLOCK * SLOTS
    r, i = iota((height, wide), 0), iota((height, wide), 1)
    peer, j = r >> 3, r & (BLOCK - 1)
    main = ((i == peer * SLOTS + j) & (j < SLOTS)).astype(F32).astype(BF)
    for g in range(parts):
        rows = slice(g * wide, (g + 1) * wide)
        tail = rows_ref[rows, section(SECTIONS)]
        for k in range(SECTIONS):
            last = ((i == peer * SLOTS + (j - SLOTS) * 3 + k) & (j >= SLOTS)).astype(F32).astype(BF)
            block_ref[g * height : (g + 1) * height, section(k)] = (
                dot(main, rows_ref[rows, section(k)]) + dot(last, tail)
            ).astype(BF)


def forward_kernel(order_ref, block_ref, *refs):
    *shards, weights_hbm, factor_hbm, weights_ref, factor_ref, rows_ref, sems = refs
    hidden = factor_ref.shape[1] // 2
    copies = []
    for n, shard in enumerate(shards):
        rows = pl.ds(pl.multiple_of(order_ref[n], LANES), shard.shape[0])
        copies.append(pltpu.make_async_copy(shard, weights_ref.at[rows], sems.at[n]))
    for copy in copies:
        copy.start()
    unpack_blocks(block_ref, rows_ref)
    for copy in copies:
        copy.wait()
    keep = [
        pltpu.make_async_copy(weights_ref, weights_hbm, sems.at[len(shards)]),
        pltpu.make_async_copy(factor_ref, factor_hbm, sems.at[len(shards) + 1]),
    ]
    keep[0].start()
    gate_pre = dot(rows_ref[...], weights_ref[:, :hidden])
    up_pre = dot(rows_ref[...], weights_ref[:, hidden : 2 * hidden])
    s = jax.nn.sigmoid(gate_pre)
    factor_ref[:, :hidden] = up_pre * s * (1.0 + gate_pre * (1.0 - s))
    factor_ref[:, hidden:] = gate_pre * s
    keep[1].start()
    for copy in keep:
        copy.wait()


def backward_kernel(
    block_hbm, weights_hbm, factor_hbm, out_ref, block_ref, weights_ref, factor_ref, rows_ref, hidden_ref, sems
):
    hidden = factor_ref.shape[1] // 2
    down, rest = slice(2 * hidden, 3 * hidden), slice(0, 2 * hidden)
    copies = [
        pltpu.make_async_copy(source, target, sems.at[n])
        for n, (source, target) in enumerate(
            (
                (block_hbm, block_ref),
                (weights_hbm.at[:, down], weights_ref.at[:, down]),
                (factor_hbm, factor_ref),
                (weights_hbm.at[:, rest], weights_ref.at[:, rest]),
            )
        )
    ]
    copies[0].start()
    copies[1].start()
    copies[0].wait()
    copies[2].start()
    copies[3].start()
    unpack_blocks(block_ref, rows_ref)
    copies[1].wait()
    back = dot(rows_ref[...], weights_ref[:, down])
    copies[2].wait()
    hidden_ref[:, :hidden] = (back * factor_ref[:, :hidden]).astype(BF)
    hidden_ref[:, hidden:] = (back * factor_ref[:, hidden:]).astype(BF)
    copies[3].wait()
    for k in range(SECTIONS + 1):
        rows_ref[:, section(k)] = dot_last(hidden_ref[...], weights_ref[section(k), rest]).astype(BF)
    pack_blocks(rows_ref, out_ref)


def finish_kernel(
    block_ref, residual_ref, gain_ref, q_ref, units_ref, token_ref, out_ref, grad_ref
):
    total, q = block_ref.shape[0], q_ref[...]
    gates = units_ref[...].astype(F32) * (1.0 / 256.0)
    first, second = gates[0:1], gates[1:2]
    tokens = q.shape[1]
    main = picks(total, q, first, second)
    tail = jnp.zeros((tokens, SECTION), F32)
    for k in range(SECTIONS):
        both = dot_first(
            jnp.concatenate([main, picks(total, tail_row(q, k), first, second)], axis=1),
            block_ref[:, section(k)],
        )
        grad_ref[:, section(k)] = both[:tokens]
        tail = tail + both[tokens:]
    grad_ref[:, section(SECTIONS)] = tail
    stream = residual_ref[...].astype(F32)
    root = inverse_rms(stream)
    gain = gain_ref[...].astype(F32)
    for c in range(gain.shape[0]):
        lanes = slice(c * LANES, (c + 1) * LANES)
        grad_ref[:, lanes] = gain[c : c + 1] * grad_ref[:, lanes]
    scaled = grad_ref[...]
    correction = jnp.mean(scaled * stream, axis=-1, keepdims=True)
    cot = token_ref[...].astype(F32)
    out_ref[...] = (cot + root * scaled - stream * (root * root * root * correction)).astype(BF)


def params(mib):
    return pltpu.CompilerParams(vmem_limit_bytes=mib << 20)


IN_SMEM = pl.BlockSpec(memory_space=pltpu.SMEM)
IN_VMEM = pl.BlockSpec(memory_space=pltpu.VMEM)
IN_HBM = pl.BlockSpec(memory_space=pltpu.HBM)


def hbm(value):
    return pltpu.with_memory_space_constraint(value, pltpu.HBM)


def per_device(
    query_reps,
    code_reps,
    positives,
    file_lengths,
    residual,
    norm_gain,
    expert_ids,
    gate_units,
    w_gate,
    w_up,
    w_down,
):
    owners = lax.axis_size("expert")
    columns = code_reps.shape[0]
    queries, width = query_reps.shape
    files = file_lengths.shape[2]
    tokens = residual.shape[1]
    hidden = w_gate.shape[2]
    total = owners * BLOCK
    lengths = file_lengths.reshape(1, files)
    stream = residual[0]
    gain = norm_gain.reshape(width // LANES, LANES)
    ids = expert_ids[0].T
    units = gate_units[0].T

    owner = lax.axis_index("expert")[None]
    half = w_gate.shape[1] // 2

    def exchange(value):
        shape = value.shape
        return lax.all_to_all(
            value.reshape(owners, BLOCK, shape[1]), "expert", 0, 0, tiled=True
        ).reshape(shape)

    blocks, scores, q, local_top, local_rest, upper, lower = pl.pallas_call(
        functools.partial(dispatch_kernel, experts=owners),
        out_shape=(
            pltpu.HBM((total, BLOCK_WIDTH + LANES), BF),
            pltpu.HBM((columns, queries), F32),
            jax.ShapeDtypeStruct((2, tokens), jnp.int32),
            jax.ShapeDtypeStruct((1, queries), F32),
            jax.ShapeDtypeStruct((1, queries), F32),
            jax.ShapeDtypeStruct((half, 3 * hidden), BF),
            jax.ShapeDtypeStruct((half, 3 * hidden), BF),
        ),
        in_specs=[IN_SMEM] + [IN_HBM] * 9,
        out_specs=(IN_HBM, IN_HBM) + (IN_VMEM,) * 5,
        scratch_shapes=[
            pltpu.VMEM((2, tokens), jnp.int32),
            pltpu.VMEM((tokens, width), BF),
            pltpu.VMEM(gain.shape, BF),
            pltpu.VMEM((columns, width), BF),
            pltpu.VMEM((1, queries), jnp.int32),
            pltpu.VMEM((queries, width), BF),
            pltpu.VMEM((columns, queries), F32),
            pltpu.VMEM((tokens, width), BF),
            pltpu.VMEM((total, BLOCK_WIDTH + LANES), BF),
            pltpu.SemaphoreType.DMA((PIECES + 13 + SECTIONS,)),
        ],
        compiler_params=params(16),
        name="dispatch",
    )(
        owner,
        hbm(ids),
        hbm(stream),
        hbm(gain),
        hbm(code_reps),
        hbm(positives[None]),
        hbm(query_reps),
        hbm(w_gate[0]),
        hbm(w_up[0]),
        hbm(w_down[0]),
    )
    size = lax.axis_size("dp")
    me = lax.axis_index("dp")

    def ahead(value, step):
        return lax.ppermute(value, "dp", [(d, (d + step) % size) for d in range(size)])

    def partner(value):
        return lax.ppermute(value, "dp", [(d, d ^ 1) for d in range(size)])

    left, right = 2, size - 2
    upper_left, lower_right = ahead(upper, left), ahead(lower, right)
    lower_left, upper_right = ahead(lower, left), ahead(upper, right)
    partner_upper, partner_lower = partner(upper), partner(lower)
    moved = [upper_left, lower_right, lower_left, upper_right, partner_upper, partner_lower]
    blocks = exchange(blocks)
    parts = pl.pallas_call(
        weights_kernel,
        out_shape=jax.ShapeDtypeStruct((columns, width), BF),
        in_specs=[IN_VMEM, IN_SMEM] + [IN_VMEM] * 3 + [IN_HBM] * (2 + len(moved)),
        out_specs=IN_VMEM,
        scratch_shapes=[
            pltpu.VMEM((total, LANES), F32),
            pltpu.VMEM((columns, queries), BF),
            pltpu.VMEM((columns, queries), F32),
            pltpu.VMEM((queries, width), BF),
            pltpu.SemaphoreType.DMA((PIECES + 1,)),
        ],
        compiler_params=params(12),
        name="code_weights",
    )(
        blocks,
        owner,
        local_top,
        local_rest,
        positives[None],
        hbm(scores),
        hbm(query_reps),
        *[hbm(shard) for shard in moved],
    )
    parts = lax.all_to_all(
        parts.reshape(columns // files, files, width), "dp", 0, 0, tiled=True
    ).reshape(columns, width)
    cot_blocks, token_cot = pl.pallas_call(
        cotangent_kernel,
        out_shape=(
            pltpu.HBM((total, BLOCK_WIDTH), BF),
            pltpu.HBM((tokens, width), BF),
        ),
        in_specs=[IN_VMEM, IN_SMEM, IN_VMEM],
        out_specs=(IN_HBM, IN_HBM),
        scratch_shapes=[
            pltpu.VMEM((tokens, width), BF),
            pltpu.VMEM((total, BLOCK_WIDTH), BF),
            pltpu.SemaphoreType.DMA((SECTIONS + 1,)),
        ],
        compiler_params=params(12),
        name="cotangent",
    )(parts, lengths, q)
    cot_blocks = exchange(cot_blocks)
    moved = lax.optimization_barrier((*moved, parts))[:-1]
    upper_left, lower_right, lower_left, upper_right, partner_upper, partner_lower = moved
    shards = [upper_left, lower_left, upper_right, lower_right, ahead(upper_left, left), ahead(lower_right, right)]
    shards += [partner(shard) for shard in shards]
    shards = [hbm(shard) for shard in (upper, lower, partner_upper, partner_lower, *shards)]
    places = [(d, 0, start) for d in (me, me ^ 1) for start in (0, half)]
    places += [
        (d, step, start) for d in (me, me ^ 1) for step in (size - 2, 2, 4) for start in (0, half)
    ]
    order = jnp.stack(
        [jnp.bitwise_and(d + step, size - 1) * (2 * half) + start for d, step, start in places]
    ).astype(jnp.int32)

    rows = owners * SLOTS
    weights, factor = pl.pallas_call(
        forward_kernel,
        out_shape=(pltpu.HBM((width, 3 * hidden), BF), pltpu.HBM((rows, 2 * hidden), F32)),
        in_specs=[IN_SMEM, IN_VMEM] + [IN_HBM] * len(shards),
        out_specs=(IN_HBM, IN_HBM),
        scratch_shapes=[
            pltpu.VMEM((width, 3 * hidden), BF),
            pltpu.VMEM((rows, 2 * hidden), F32),
            pltpu.VMEM((rows, width), BF),
            pltpu.SemaphoreType.DMA((len(shards) + 2,)),
        ],
        compiler_params=params(32),
        name="expert_forward",
    )(order, blocks, *shards)
    result = pl.pallas_call(
        backward_kernel,
        out_shape=jax.ShapeDtypeStruct((total, BLOCK_WIDTH), BF),
        in_specs=[IN_HBM] * 3,
        out_specs=IN_VMEM,
        scratch_shapes=[
            pltpu.VMEM((total, BLOCK_WIDTH), BF),
            pltpu.VMEM((width, 3 * hidden), BF),
            pltpu.VMEM((rows, 2 * hidden), F32),
            pltpu.VMEM((rows, width), BF),
            pltpu.VMEM((rows, 2 * hidden), BF),
            pltpu.SemaphoreType.DMA((4,)),
        ],
        compiler_params=params(32),
        name="expert_backward",
    )(hbm(cot_blocks), hbm(weights), hbm(factor))

    token_grad = pl.pallas_call(
        finish_kernel,
        out_shape=jax.ShapeDtypeStruct((tokens, width), BF),
        in_specs=[IN_VMEM] * 6,
        out_specs=IN_VMEM,
        scratch_shapes=[pltpu.VMEM((tokens, width), F32)],
        compiler_params=params(12),
        name="finish",
    )(exchange(result), stream, gain, q, units, token_cot)
    return token_grad[None]


def solution(mesh):
    return jax.shard_map(
        per_device,
        mesh=mesh,
        in_specs=(
            P("dp", None),
            P("expert", None),
            P("dp"),
            P("expert", "dp", None),
            P("expert", "dp", None),
            P(),
            P("expert", "dp", None),
            P("expert", "dp", None),
            P("expert", "dp", None),
            P("expert", "dp", None),
            P("expert", "dp", None),
        ),
        out_specs=P("expert", "dp", None),
        check_vma=False,
    )
```

```python
import functools
import jax
import jax.numpy as jnp
from jax import lax
from jax.experimental import pallas as pl
from jax.experimental.pallas import tpu as pltpu
from jax.sharding import PartitionSpec as P

SCORE_SCALE = 20.0
GRAD_SCALE = 2560.0
EPSILON = 1e-06
BF = jnp.bfloat16
F32 = jnp.float32

SLOTS = 6
BLOCK = 8
SECTION = 512
SECTIONS = 3
BLOCK_WIDTH = SECTIONS * SECTION
LANES = 128
PIECES = 4


def iota(shape, dim):
    return lax.broadcasted_iota(jnp.int32, shape, dim)


def dot(a, b):
    return jnp.dot(a, b, preferred_element_type=F32)


def dot_first(a, b):
    return lax.dot_general(a, b, (((0,), (0,)), ((), ())), preferred_element_type=F32)


def dot_last(a, b):
    return lax.dot_general(a, b, (((1,), (1,)), ((), ())), preferred_element_type=F32)


def section(k):
    return slice(k * SECTION, (k + 1) * SECTION)


def tail_row(q, k):
    rank = jnp.bitwise_and(q, BLOCK - 1)
    high = (rank >= 3).astype(jnp.int32)
    return jnp.where(rank - 3 * high == k, q - rank + SLOTS + high, -1)


def picks(rows, q, first, second):
    r = iota((rows, q.shape[1]), 0)
    zero = jnp.zeros((), F32)
    return (jnp.where(r == q[0:1], first, zero) + jnp.where(r == q[1:2], second, zero)).astype(BF)


def pack_rows(rows_ref, q, stage_ref, out_hbm, sems):
    total = stage_ref.shape[0]
    main = picks(total, q, 1.0, 1.0)
    tail = rows_ref[:, section(SECTIONS)]
    copies = []
    for k in range(SECTIONS):
        left = jnp.concatenate([main, picks(total, tail_row(q, k), 1.0, 1.0)], axis=1)
        right = jnp.concatenate([rows_ref[:, section(k)], tail], axis=0)
        stage_ref[:, section(k)] = dot(left, right).astype(BF)
        copies.append(
            pltpu.make_async_copy(stage_ref.at[:, section(k)], out_hbm.at[:, section(k)], sems.at[k])
        )
        copies[-1].start()
    return copies


def inverse_rms(stream):
    return lax.rsqrt(jnp.mean(stream * stream, axis=-1, keepdims=True) + EPSILON)


def dispatch_kernel(
    owner_ref,
    ids_hbm,
    residual_hbm,
    gain_hbm,
    code_hbm,
    positives_hbm,
    query_hbm,
    w0_hbm,
    w1_hbm,
    w2_hbm,
    out_hbm,
    scores_hbm,
    q_ref,
    top_ref,
    rest_ref,
    joined_a_ref,
    joined_b_ref,
    ids_ref,
    residual_ref,
    gain_ref,
    code_ref,
    positives_ref,
    query_ref,
    scores_ref,
    normed_ref,
    stage_ref,
    sems,
    *,
    experts,
):
    hidden, columns = w0_hbm.shape[1], code_ref.shape[0]
    base = PIECES + 8 + SECTIONS
    inputs = [
        pltpu.make_async_copy(source, target, sems.at[base + n])
        for n, (source, target) in enumerate(
            (
                (ids_hbm, ids_ref),
                (residual_hbm, residual_ref),
                (gain_hbm, gain_ref),
                (code_hbm, code_ref),
                (positives_hbm, positives_ref),
            )
        )
    ]
    for copy in inputs:
        copy.start()
    parts = [slice(c * LANES, (c + 1) * LANES) for c in range(PIECES)]
    queries = [
        pltpu.make_async_copy(query_hbm.at[part], query_ref.at[part], sems.at[c])
        for c, part in enumerate(parts)
    ]
    for copy in queries:
        copy.start()
    half = joined_a_ref.shape[0]
    copies = [
        pltpu.make_async_copy(
            w_hbm.at[n * half : (n + 1) * half],
            joined_ref.at[:, k * hidden : (k + 1) * hidden],
            sems.at[PIECES + 2 * k + n],
        )
        for k, w_hbm in enumerate((w0_hbm, w1_hbm, w2_hbm))
        for n, joined_ref in enumerate((joined_a_ref, joined_b_ref))
    ]
    for copy in inputs:
        copy.wait()
    for copy in copies:
        copy.start()
    stream = residual_ref[...].astype(F32)
    scaled = stream * inverse_rms(stream)
    gain = gain_ref[...].astype(F32)
    for c in range(gain.shape[0]):
        lanes = slice(c * LANES, (c + 1) * LANES)
        normed_ref[:, lanes] = (scaled[:, lanes] * gain[c : c + 1]).astype(BF)
    ids = jnp.concatenate([ids_ref[0:1, :], ids_ref[1:2, :]], axis=1)
    count = ids.shape[1]
    table = (iota((experts, count), 0) == ids).astype(F32)
    earlier = dot(
        table.astype(BF), (iota((count, count), 0) < iota((count, count), 1)).astype(F32).astype(BF)
    )
    rank = jnp.sum(table * earlier, axis=0, keepdims=True).astype(jnp.int32)
    q_flat = ids * BLOCK + rank
    q = jnp.concatenate([q_flat[:, : count // 2], q_flat[:, count // 2 :]], axis=0)
    q_ref[...] = q
    copies += pack_rows(normed_ref, q, stage_ref, out_hbm, sems.at[PIECES + 6 : PIECES + 6 + SECTIONS])
    column = owner_ref[0] * columns + iota((columns, 1), 0)
    high, low = [], []
    for copy, part in zip(queries, parts):
        copy.wait()
        scores = dot_last(code_ref[...], query_ref[part, :]) * SCORE_SCALE
        scores_ref[:, part] = scores
        top = jnp.max(scores, axis=0, keepdims=True)
        exponent = jnp.exp(scores - top)
        top_ref[:, part] = top
        rest_ref[:, part] = jnp.sum(
            jnp.where(positives_ref[:, part] == column, 0.0, exponent), axis=0, keepdims=True
        )
        log_sum = top + jnp.log(jnp.sum(exponent, axis=0, keepdims=True))
        high.append(log_sum.astype(BF).astype(F32))
        low.append(log_sum - high[-1])
    pieces = jnp.concatenate(high + low, axis=0)
    stage_ref[:, BLOCK_WIDTH:] = jnp.concatenate([pieces] * experts, axis=0).astype(BF)
    first = PIECES + 6 + SECTIONS
    copies += [
        pltpu.make_async_copy(stage_ref.at[:, BLOCK_WIDTH:], out_hbm.at[:, BLOCK_WIDTH:], sems.at[first]),
        pltpu.make_async_copy(scores_ref, scores_hbm, sems.at[first + 1]),
    ]
    for copy in copies[-2:]:
        copy.start()
    for copy in copies:
        copy.wait()


def weights_kernel(
    block_ref,
    owner_ref,
    top_ref,
    rest_ref,
    positives_ref,
    scores_hbm,
    query_hbm,
    *refs,
):
    out_ref, pieces_ref, code_weights_ref, scores_ref, query_ref, sems = refs[-6:]
    copies = [pltpu.make_async_copy(scores_hbm, scores_ref, sems.at[PIECES])]
    copies += [
        pltpu.make_async_copy(
            query_hbm.at[c * LANES : (c + 1) * LANES], query_ref.at[c * LANES : (c + 1) * LANES], sems.at[c]
        )
        for c in range(PIECES)
    ]
    for copy in copies:
        copy.start()
    pieces_ref[...] = block_ref[:, BLOCK_WIDTH:].astype(F32)
    peers, columns = block_ref.shape[0] // BLOCK, scores_ref.shape[0]
    owner = owner_ref[0]
    own = iota((peers, 1), 0) == owner
    column = owner * columns + iota((columns, 1), 0)
    copies[0].wait()
    for c in range(PIECES):
        lanes = slice(c * LANES, (c + 1) * LANES)
        sums = (
            pieces_ref[pl.ds(c, peers, stride=BLOCK), :]
            + pieces_ref[pl.ds(PIECES + c, peers, stride=BLOCK), :]
        )
        row_top = jnp.max(sums, axis=0, keepdims=True)
        shares = jnp.exp(sums - row_top)
        total = jnp.sum(shares, axis=0, keepdims=True)
        rest = jnp.sum(jnp.where(own, 0.0, shares), axis=0, keepdims=True)
        rest = rest + rest_ref[:, lanes] * jnp.exp(top_ref[:, lanes] - row_top)
        part = jnp.where(positives_ref[:, lanes] == column, -rest, jnp.exp(scores_ref[:, lanes] - row_top))
        code_weights_ref[:, lanes] = (part * (GRAD_SCALE / total)).astype(BF)
    for copy in copies[1:]:
        copy.wait()
    out_ref[...] = dot(code_weights_ref[...], query_ref[...]).astype(BF)


def cotangent_kernel(parts_ref, lengths_ref, q_ref, out_hbm, token_hbm, token_ref, stage_ref, sems):
    files, tokens = lengths_ref.shape[1], token_ref.shape[0]
    row, position = iota((files, 1), 0), iota((1, tokens), 1)
    length = jnp.zeros((files, 1), jnp.int32)
    segment = jnp.zeros((1, tokens), jnp.int32)
    end = jnp.int32(0)
    for f in range(files):
        length = jnp.where(row == f, lengths_ref[0, f], length)
        end = end + lengths_ref[0, f]
        segment = segment + (position >= end).astype(jnp.int32)
    code_grad = parts_ref[0:files, :].astype(F32)
    for part in range(1, parts_ref.shape[0] // files):
        code_grad = code_grad + parts_ref[part * files : (part + 1) * files, :].astype(F32)
    file_cot = (code_grad / length.astype(F32)).astype(BF)
    member = (iota((files, tokens), 0) == segment).astype(F32).astype(BF)
    token_ref[...] = dot_first(member, file_cot).astype(BF)
    keep = pltpu.make_async_copy(token_ref, token_hbm, sems.at[SECTIONS])
    keep.start()
    for copy in pack_rows(token_ref, q_ref[...], stage_ref, out_hbm, sems.at[0:SECTIONS]):
        copy.wait()
    keep.wait()


def halves(total):
    return 2 if total % 512 == 0 else 1


def unpack_blocks(block_ref, rows_ref):
    parts = halves(block_ref.shape[0])
    height = block_ref.shape[0] // parts
    wide = height // BLOCK * SLOTS
    i, r = iota((wide, height), 0), iota((wide, height), 1)
    peer, j = r >> 3, r & (BLOCK - 1)
    main = ((i == peer * SLOTS + j) & (j < SLOTS)).astype(F32).astype(BF)
    for g in range(parts):
        rows = slice(g * wide, (g + 1) * wide)
        tail = jnp.zeros((wide, SECTION), F32)
        for k in range(SECTIONS):
            last = ((i == peer * SLOTS + (j - SLOTS) * 3 + k) & (j >= SLOTS)).astype(F32).astype(BF)
            both = dot(
                jnp.concatenate([main, last], axis=0),
                block_ref[g * height : (g + 1) * height, section(k)],
            )
            rows_ref[rows, section(k)] = both[:wide].astype(BF)
            tail = tail + both[wide:]
        rows_ref[rows, section(SECTIONS)] = tail.astype(BF)


def pack_blocks(rows_ref, block_ref):
    parts = halves(block_ref.shape[0])
    height = block_ref.shape[0] // parts
    wide = height // BLOCK * SLOTS
    r, i = iota((height, wide), 0), iota((height, wide), 1)
    peer, j = r >> 3, r & (BLOCK - 1)
    main = ((i == peer * SLOTS + j) & (j < SLOTS)).astype(F32).astype(BF)
    for g in range(parts):
        rows = slice(g * wide, (g + 1) * wide)
        tail = rows_ref[rows, section(SECTIONS)]
        for k in range(SECTIONS):
            last = ((i == peer * SLOTS + (j - SLOTS) * 3 + k) & (j >= SLOTS)).astype(F32).astype(BF)
            block_ref[g * height : (g + 1) * height, section(k)] = (
                dot(main, rows_ref[rows, section(k)]) + dot(last, tail)
            ).astype(BF)


def place_rows(shards, order_ref, target_ref, columns, sems, first):
    copies = []
    for n, shard in enumerate(shards):
        rows = pl.ds(pl.multiple_of(order_ref[n], LANES), shard.shape[0])
        copies.append(pltpu.make_async_copy(shard.at[:, columns], target_ref.at[rows], sems.at[first + n]))
    return copies


def forward_kernel(order_ref, block_ref, *refs):
    *shards, weights_hbm, factor_hbm, weights_ref, factor_ref, rows_ref, sems = refs
    hidden = factor_ref.shape[1] // 2
    copies = place_rows(shards, order_ref, weights_ref, slice(0, 2 * hidden), sems, 0)
    for copy in copies:
        copy.start()
    unpack_blocks(block_ref, rows_ref)
    for copy in copies:
        copy.wait()
    keep = [
        pltpu.make_async_copy(weights_ref, weights_hbm, sems.at[len(shards)]),
        pltpu.make_async_copy(factor_ref, factor_hbm, sems.at[len(shards) + 1]),
    ]
    keep[0].start()
    gate_pre = dot(rows_ref[...], weights_ref[:, :hidden])
    up_pre = dot(rows_ref[...], weights_ref[:, hidden:])
    s = jax.nn.sigmoid(gate_pre)
    factor_ref[:, :hidden] = up_pre * s * (1.0 + gate_pre * (1.0 - s))
    factor_ref[:, hidden:] = gate_pre * s
    keep[1].start()
    for copy in keep:
        copy.wait()


def backward_kernel(order_ref, block_hbm, weights_hbm, factor_hbm, *refs):
    *shards, out_ref, block_ref, weights_ref, down_ref, factor_ref, rows_ref, hidden_ref, sems = refs
    hidden = factor_ref.shape[1] // 2
    block = pltpu.make_async_copy(block_hbm, block_ref, sems.at[0])
    factor = pltpu.make_async_copy(factor_hbm, factor_ref, sems.at[1])
    weights = pltpu.make_async_copy(weights_hbm, weights_ref, sems.at[2])
    down = place_rows(shards, order_ref, down_ref, slice(2 * hidden, 3 * hidden), sems, 3)
    block.start()
    for copy in down:
        copy.start()
    block.wait()
    factor.start()
    weights.start()
    unpack_blocks(block_ref, rows_ref)
    for copy in down:
        copy.wait()
    back = dot(rows_ref[...], down_ref[...])
    factor.wait()
    hidden_ref[:, :hidden] = (back * factor_ref[:, :hidden]).astype(BF)
    hidden_ref[:, hidden:] = (back * factor_ref[:, hidden:]).astype(BF)
    weights.wait()
    for k in range(SECTIONS + 1):
        rows_ref[:, section(k)] = dot_last(hidden_ref[...], weights_ref[section(k), :]).astype(BF)
    pack_blocks(rows_ref, out_ref)


def finish_kernel(
    block_ref, residual_ref, gain_ref, q_ref, units_ref, token_ref, out_ref, grad_ref
):
    total, q = block_ref.shape[0], q_ref[...]
    gates = units_ref[...].astype(F32) * (1.0 / 256.0)
    first, second = gates[0:1], gates[1:2]
    tokens = q.shape[1]
    main = picks(total, q, first, second)
    tail = jnp.zeros((tokens, SECTION), F32)
    for k in range(SECTIONS):
        both = dot_first(
            jnp.concatenate([main, picks(total, tail_row(q, k), first, second)], axis=1),
            block_ref[:, section(k)],
        )
        grad_ref[:, section(k)] = both[:tokens]
        tail = tail + both[tokens:]
    grad_ref[:, section(SECTIONS)] = tail
    stream = residual_ref[...].astype(F32)
    root = inverse_rms(stream)
    gain = gain_ref[...].astype(F32)
    for c in range(gain.shape[0]):
        lanes = slice(c * LANES, (c + 1) * LANES)
        grad_ref[:, lanes] = gain[c : c + 1] * grad_ref[:, lanes]
    scaled = grad_ref[...]
    correction = jnp.mean(scaled * stream, axis=-1, keepdims=True)
    cot = token_ref[...].astype(F32)
    out_ref[...] = (cot + root * scaled - stream * (root * root * root * correction)).astype(BF)


def params(mib):
    return pltpu.CompilerParams(vmem_limit_bytes=mib << 20)


IN_SMEM = pl.BlockSpec(memory_space=pltpu.SMEM)
IN_VMEM = pl.BlockSpec(memory_space=pltpu.VMEM)
IN_HBM = pl.BlockSpec(memory_space=pltpu.HBM)


def hbm(value):
    return pltpu.with_memory_space_constraint(value, pltpu.HBM)


def per_device(
    query_reps,
    code_reps,
    positives,
    file_lengths,
    residual,
    norm_gain,
    expert_ids,
    gate_units,
    w_gate,
    w_up,
    w_down,
):
    owners = lax.axis_size("expert")
    columns = code_reps.shape[0]
    queries, width = query_reps.shape
    files = file_lengths.shape[2]
    tokens = residual.shape[1]
    hidden = w_gate.shape[2]
    total = owners * BLOCK
    lengths = file_lengths.reshape(1, files)
    stream = residual[0]
    gain = norm_gain.reshape(width // LANES, LANES)
    ids = expert_ids[0].T
    units = gate_units[0].T

    owner = lax.axis_index("expert")[None]
    half = w_gate.shape[1] // 2

    def exchange(value):
        shape = value.shape
        return lax.all_to_all(
            value.reshape(owners, BLOCK, shape[1]), "expert", 0, 0, tiled=True
        ).reshape(shape)

    blocks, scores, q, local_top, local_rest, upper, lower = pl.pallas_call(
        functools.partial(dispatch_kernel, experts=owners),
        out_shape=(
            pltpu.HBM((total, BLOCK_WIDTH + LANES), BF),
            pltpu.HBM((columns, queries), F32),
            jax.ShapeDtypeStruct((2, tokens), jnp.int32),
            jax.ShapeDtypeStruct((1, queries), F32),
            jax.ShapeDtypeStruct((1, queries), F32),
            jax.ShapeDtypeStruct((half, 3 * hidden), BF),
            jax.ShapeDtypeStruct((half, 3 * hidden), BF),
        ),
        in_specs=[IN_SMEM] + [IN_HBM] * 9,
        out_specs=(IN_HBM, IN_HBM) + (IN_VMEM,) * 5,
        scratch_shapes=[
            pltpu.VMEM((2, tokens), jnp.int32),
            pltpu.VMEM((tokens, width), BF),
            pltpu.VMEM(gain.shape, BF),
            pltpu.VMEM((columns, width), BF),
            pltpu.VMEM((1, queries), jnp.int32),
            pltpu.VMEM((queries, width), BF),
            pltpu.VMEM((columns, queries), F32),
            pltpu.VMEM((tokens, width), BF),
            pltpu.VMEM((total, BLOCK_WIDTH + LANES), BF),
            pltpu.SemaphoreType.DMA((PIECES + 13 + SECTIONS,)),
        ],
        compiler_params=params(16),
        name="dispatch",
    )(
        owner,
        hbm(ids),
        hbm(stream),
        hbm(gain),
        hbm(code_reps),
        hbm(positives[None]),
        hbm(query_reps),
        hbm(w_gate[0]),
        hbm(w_up[0]),
        hbm(w_down[0]),
    )
    size = lax.axis_size("dp")
    me = lax.axis_index("dp")

    def ahead(value, step):
        return lax.ppermute(value, "dp", [(d, (d + step) % size) for d in range(size)])

    def partner(value):
        return lax.ppermute(value, "dp", [(d, d ^ 1) for d in range(size)])

    left, right = 2, size - 2
    upper_left, lower_right = ahead(upper, left), ahead(lower, right)
    lower_left, upper_right = ahead(lower, left), ahead(upper, right)
    partner_upper, partner_lower = partner(upper), partner(lower)
    partner_upper_left, partner_upper_right = partner(upper_left), partner(upper_right)
    moved = [upper_left, lower_right, lower_left, upper_right, partner_upper, partner_lower]
    moved += [partner_upper_left, partner_upper_right]
    blocks = exchange(blocks)
    parts = pl.pallas_call(
        weights_kernel,
        out_shape=jax.ShapeDtypeStruct((columns, width), BF),
        in_specs=[IN_VMEM, IN_SMEM] + [IN_VMEM] * 3 + [IN_HBM] * (2 + len(moved)),
        out_specs=IN_VMEM,
        scratch_shapes=[
            pltpu.VMEM((total, LANES), F32),
            pltpu.VMEM((columns, queries), BF),
            pltpu.VMEM((columns, queries), F32),
            pltpu.VMEM((queries, width), BF),
            pltpu.SemaphoreType.DMA((PIECES + 1,)),
        ],
        compiler_params=params(12),
        name="code_weights",
    )(
        blocks,
        owner,
        local_top,
        local_rest,
        positives[None],
        hbm(scores),
        hbm(query_reps),
        *[hbm(shard) for shard in moved],
    )
    parts = lax.all_to_all(
        parts.reshape(columns // files, files, width), "dp", 0, 0, tiled=True
    ).reshape(columns, width)
    cot_blocks, token_cot = pl.pallas_call(
        cotangent_kernel,
        out_shape=(
            pltpu.HBM((total, BLOCK_WIDTH), BF),
            pltpu.HBM((tokens, width), BF),
        ),
        in_specs=[IN_VMEM, IN_SMEM, IN_VMEM],
        out_specs=(IN_HBM, IN_HBM),
        scratch_shapes=[
            pltpu.VMEM((tokens, width), BF),
            pltpu.VMEM((total, BLOCK_WIDTH), BF),
            pltpu.SemaphoreType.DMA((SECTIONS + 1,)),
        ],
        compiler_params=params(12),
        name="cotangent",
    )(parts, lengths, q)
    cot_blocks = exchange(cot_blocks)
    moved = lax.optimization_barrier((*moved, parts))[:-1]
    upper_left, lower_right, lower_left, upper_right, partner_upper, partner_lower = moved[:6]
    partner_upper_left, partner_upper_right = moved[6:]
    upper_across, lower_across = ahead(upper_left, left), ahead(lower_right, right)
    shards = [upper, lower, partner_upper, partner_lower]
    shards += [upper_left, lower_left, upper_right, lower_right, upper_across, lower_across]
    shards += [partner_upper_left, partner(lower_left), partner_upper_right, partner(lower_right)]
    shards += [partner(upper_across), partner(lower_across)]
    shards = [hbm(shard) for shard in shards]
    places = [(d, 0, start) for d in (me, me ^ 1) for start in (0, half)]
    places += [
        (d, step, start) for d in (me, me ^ 1) for step in (size - 2, 2, 4) for start in (0, half)
    ]
    order = jnp.stack(
        [jnp.bitwise_and(d + step, size - 1) * (2 * half) + start for d, step, start in places]
    ).astype(jnp.int32)

    rows = owners * SLOTS
    weights, factor = pl.pallas_call(
        forward_kernel,
        out_shape=(pltpu.HBM((width, 2 * hidden), BF), pltpu.HBM((rows, 2 * hidden), F32)),
        in_specs=[IN_SMEM, IN_VMEM] + [IN_HBM] * len(shards),
        out_specs=(IN_HBM, IN_HBM),
        scratch_shapes=[
            pltpu.VMEM((width, 2 * hidden), BF),
            pltpu.VMEM((rows, 2 * hidden), F32),
            pltpu.VMEM((rows, width), BF),
            pltpu.SemaphoreType.DMA((len(shards) + 2,)),
        ],
        compiler_params=params(32),
        name="expert_forward",
    )(order, blocks, *shards)
    result = pl.pallas_call(
        backward_kernel,
        out_shape=jax.ShapeDtypeStruct((total, BLOCK_WIDTH), BF),
        in_specs=[IN_SMEM] + [IN_HBM] * (3 + len(shards)),
        out_specs=IN_VMEM,
        scratch_shapes=[
            pltpu.VMEM((total, BLOCK_WIDTH), BF),
            pltpu.VMEM((width, 2 * hidden), BF),
            pltpu.VMEM((width, hidden), BF),
            pltpu.VMEM((rows, 2 * hidden), F32),
            pltpu.VMEM((rows, width), BF),
            pltpu.VMEM((rows, 2 * hidden), BF),
            pltpu.SemaphoreType.DMA((len(shards) + 3,)),
        ],
        compiler_params=params(32),
        name="expert_backward",
    )(order, hbm(cot_blocks), hbm(weights), hbm(factor), *shards)

    token_grad = pl.pallas_call(
        finish_kernel,
        out_shape=jax.ShapeDtypeStruct((tokens, width), BF),
        in_specs=[IN_VMEM] * 6,
        out_specs=IN_VMEM,
        scratch_shapes=[pltpu.VMEM((tokens, width), F32)],
        compiler_params=params(12),
        name="finish",
    )(exchange(result), stream, gain, q, units, token_cot)
    return token_grad[None]


def solution(mesh):
    return jax.shard_map(
        per_device,
        mesh=mesh,
        in_specs=(
            P("dp", None),
            P("expert", None),
            P("dp"),
            P("expert", "dp", None),
            P("expert", "dp", None),
            P(),
            P("expert", "dp", None),
            P("expert", "dp", None),
            P("expert", "dp", None),
            P("expert", "dp", None),
            P("expert", "dp", None),
        ),
        out_specs=P("expert", "dp", None),
        check_vma=False,
    )
```

```python
import functools
import jax
import jax.numpy as jnp
from jax import lax
from jax.experimental import pallas as pl
from jax.experimental.pallas import tpu as pltpu
from jax.sharding import PartitionSpec as P

SCORE_SCALE = 20.0
GRAD_SCALE = 2560.0
EPSILON = 1e-06
BF = jnp.bfloat16
F32 = jnp.float32

SLOTS = 6
BLOCK = 8
SECTION = 512
SECTIONS = 3
BLOCK_WIDTH = SECTIONS * SECTION
LANES = 128
PIECES = 4


def iota(shape, dim):
    return lax.broadcasted_iota(jnp.int32, shape, dim)


def dot(a, b):
    return jnp.dot(a, b, preferred_element_type=F32)


def dot_first(a, b):
    return lax.dot_general(a, b, (((0,), (0,)), ((), ())), preferred_element_type=F32)


def dot_last(a, b):
    return lax.dot_general(a, b, (((1,), (1,)), ((), ())), preferred_element_type=F32)


def section(k):
    return slice(k * SECTION, (k + 1) * SECTION)


def tail_row(q, k):
    rank = jnp.bitwise_and(q, BLOCK - 1)
    high = (rank >= 3).astype(jnp.int32)
    return jnp.where(rank - 3 * high == k, q - rank + SLOTS + high, -1)


def picks(rows, q, first, second):
    r = iota((rows, q.shape[1]), 0)
    zero = jnp.zeros((), F32)
    return (jnp.where(r == q[0:1], first, zero) + jnp.where(r == q[1:2], second, zero)).astype(BF)


def pack_rows(rows_ref, q, stage_ref, out_hbm, sems):
    total = stage_ref.shape[0]
    main = picks(total, q, 1.0, 1.0)
    tail = rows_ref[:, section(SECTIONS)]
    copies = []
    for k in range(SECTIONS):
        left = jnp.concatenate([main, picks(total, tail_row(q, k), 1.0, 1.0)], axis=1)
        right = jnp.concatenate([rows_ref[:, section(k)], tail], axis=0)
        stage_ref[:, section(k)] = dot(left, right).astype(BF)
        copies.append(
            pltpu.make_async_copy(stage_ref.at[:, section(k)], out_hbm.at[:, section(k)], sems.at[k])
        )
        copies[-1].start()
    return copies


def inverse_rms(stream):
    return lax.rsqrt(jnp.mean(stream * stream, axis=-1, keepdims=True) + EPSILON)


def dispatch_kernel(
    owner_ref,
    ids_hbm,
    residual_hbm,
    gain_hbm,
    code_hbm,
    positives_hbm,
    query_hbm,
    w0_hbm,
    w1_hbm,
    w2_hbm,
    out_hbm,
    scores_hbm,
    q_ref,
    top_ref,
    rest_ref,
    joined_a_ref,
    joined_b_ref,
    ids_ref,
    residual_ref,
    gain_ref,
    code_ref,
    positives_ref,
    query_ref,
    scores_ref,
    normed_ref,
    stage_ref,
    sems,
    *,
    experts,
):
    hidden, columns = w0_hbm.shape[1], code_ref.shape[0]
    base = PIECES + 8 + SECTIONS
    inputs = [
        pltpu.make_async_copy(source, target, sems.at[base + n])
        for n, (source, target) in enumerate(
            (
                (ids_hbm, ids_ref),
                (residual_hbm, residual_ref),
                (gain_hbm, gain_ref),
                (code_hbm, code_ref),
                (positives_hbm, positives_ref),
            )
        )
    ]
    for copy in inputs:
        copy.start()
    parts = [slice(c * LANES, (c + 1) * LANES) for c in range(PIECES)]
    queries = [
        pltpu.make_async_copy(query_hbm.at[part], query_ref.at[part], sems.at[c])
        for c, part in enumerate(parts)
    ]
    for copy in queries:
        copy.start()
    half = joined_a_ref.shape[0]
    copies = [
        pltpu.make_async_copy(
            w_hbm.at[n * half : (n + 1) * half],
            joined_ref.at[:, k * hidden : (k + 1) * hidden],
            sems.at[PIECES + 2 * k + n],
        )
        for k, w_hbm in enumerate((w0_hbm, w1_hbm, w2_hbm))
        for n, joined_ref in enumerate((joined_a_ref, joined_b_ref))
    ]
    for copy in inputs:
        copy.wait()
    for copy in copies:
        copy.start()
    stream = residual_ref[...].astype(F32)
    scaled = stream * inverse_rms(stream)
    gain = gain_ref[...].astype(F32)
    for c in range(gain.shape[0]):
        lanes = slice(c * LANES, (c + 1) * LANES)
        normed_ref[:, lanes] = (scaled[:, lanes] * gain[c : c + 1]).astype(BF)
    ids = jnp.concatenate([ids_ref[0:1, :], ids_ref[1:2, :]], axis=1)
    count = ids.shape[1]
    table = (iota((experts, count), 0) == ids).astype(F32)
    earlier = dot(
        table.astype(BF), (iota((count, count), 0) < iota((count, count), 1)).astype(F32).astype(BF)
    )
    rank = jnp.sum(table * earlier, axis=0, keepdims=True).astype(jnp.int32)
    q_flat = ids * BLOCK + rank
    q = jnp.concatenate([q_flat[:, : count // 2], q_flat[:, count // 2 :]], axis=0)
    q_ref[...] = q
    copies += pack_rows(normed_ref, q, stage_ref, out_hbm, sems.at[PIECES + 6 : PIECES + 6 + SECTIONS])
    column = owner_ref[0] * columns + iota((columns, 1), 0)
    high, low = [], []
    for copy, part in zip(queries, parts):
        copy.wait()
        scores = dot_last(code_ref[...], query_ref[part, :]) * SCORE_SCALE
        scores_ref[:, part] = scores
        top = jnp.max(scores, axis=0, keepdims=True)
        exponent = jnp.exp(scores - top)
        top_ref[:, part] = top
        rest_ref[:, part] = jnp.sum(
            jnp.where(positives_ref[:, part] == column, 0.0, exponent), axis=0, keepdims=True
        )
        log_sum = top + jnp.log(jnp.sum(exponent, axis=0, keepdims=True))
        high.append(log_sum.astype(BF).astype(F32))
        low.append(log_sum - high[-1])
    pieces = jnp.concatenate(high + low, axis=0)
    stage_ref[:, BLOCK_WIDTH:] = jnp.concatenate([pieces] * experts, axis=0).astype(BF)
    first = PIECES + 6 + SECTIONS
    copies += [
        pltpu.make_async_copy(stage_ref.at[:, BLOCK_WIDTH:], out_hbm.at[:, BLOCK_WIDTH:], sems.at[first]),
        pltpu.make_async_copy(scores_ref, scores_hbm, sems.at[first + 1]),
    ]
    for copy in copies[-2:]:
        copy.start()
    for copy in copies:
        copy.wait()


def weights_kernel(
    block_ref,
    owner_ref,
    top_ref,
    rest_ref,
    positives_ref,
    scores_hbm,
    query_hbm,
    *refs,
):
    out_ref, pieces_ref, code_weights_ref, scores_ref, query_ref, sems = refs[-6:]
    copies = [pltpu.make_async_copy(scores_hbm, scores_ref, sems.at[PIECES])]
    copies += [
        pltpu.make_async_copy(
            query_hbm.at[c * LANES : (c + 1) * LANES], query_ref.at[c * LANES : (c + 1) * LANES], sems.at[c]
        )
        for c in range(PIECES)
    ]
    for copy in copies:
        copy.start()
    pieces_ref[...] = block_ref[:, BLOCK_WIDTH:].astype(F32)
    peers, columns = block_ref.shape[0] // BLOCK, scores_ref.shape[0]
    owner = owner_ref[0]
    own = iota((peers, 1), 0) == owner
    column = owner * columns + iota((columns, 1), 0)
    copies[0].wait()
    for c in range(PIECES):
        lanes = slice(c * LANES, (c + 1) * LANES)
        sums = (
            pieces_ref[pl.ds(c, peers, stride=BLOCK), :]
            + pieces_ref[pl.ds(PIECES + c, peers, stride=BLOCK), :]
        )
        row_top = jnp.max(sums, axis=0, keepdims=True)
        shares = jnp.exp(sums - row_top)
        total = jnp.sum(shares, axis=0, keepdims=True)
        rest = jnp.sum(jnp.where(own, 0.0, shares), axis=0, keepdims=True)
        rest = rest + rest_ref[:, lanes] * jnp.exp(top_ref[:, lanes] - row_top)
        part = jnp.where(positives_ref[:, lanes] == column, -rest, jnp.exp(scores_ref[:, lanes] - row_top))
        code_weights_ref[:, lanes] = (part * (GRAD_SCALE / total)).astype(BF)
    for copy in copies[1:]:
        copy.wait()
    out_ref[...] = dot(code_weights_ref[...], query_ref[...]).astype(BF)


def cotangent_kernel(parts_ref, lengths_ref, q_ref, out_hbm, token_hbm, token_ref, stage_ref, sems):
    files, tokens = lengths_ref.shape[1], token_ref.shape[0]
    row, position = iota((files, 1), 0), iota((1, tokens), 1)
    length = jnp.zeros((files, 1), jnp.int32)
    segment = jnp.zeros((1, tokens), jnp.int32)
    end = jnp.int32(0)
    for f in range(files):
        length = jnp.where(row == f, lengths_ref[0, f], length)
        end = end + lengths_ref[0, f]
        segment = segment + (position >= end).astype(jnp.int32)
    code_grad = parts_ref[0:files, :].astype(F32)
    for part in range(1, parts_ref.shape[0] // files):
        code_grad = code_grad + parts_ref[part * files : (part + 1) * files, :].astype(F32)
    file_cot = (code_grad / length.astype(F32)).astype(BF)
    member = (iota((files, tokens), 0) == segment).astype(F32).astype(BF)
    token_ref[...] = dot_first(member, file_cot).astype(BF)
    keep = pltpu.make_async_copy(token_ref, token_hbm, sems.at[SECTIONS])
    keep.start()
    for copy in pack_rows(token_ref, q_ref[...], stage_ref, out_hbm, sems.at[0:SECTIONS]):
        copy.wait()
    keep.wait()


def halves(total):
    return 2 if total % 512 == 0 else 1


def unpack_blocks(block_ref, rows_ref):
    parts = halves(block_ref.shape[0])
    height = block_ref.shape[0] // parts
    wide = height // BLOCK * SLOTS
    i, r = iota((wide, height), 0), iota((wide, height), 1)
    peer, j = r >> 3, r & (BLOCK - 1)
    main = ((i == peer * SLOTS + j) & (j < SLOTS)).astype(F32).astype(BF)
    for g in range(parts):
        rows = slice(g * wide, (g + 1) * wide)
        tail = jnp.zeros((wide, SECTION), F32)
        for k in range(SECTIONS):
            last = ((i == peer * SLOTS + (j - SLOTS) * 3 + k) & (j >= SLOTS)).astype(F32).astype(BF)
            both = dot(
                jnp.concatenate([main, last], axis=0),
                block_ref[g * height : (g + 1) * height, section(k)],
            )
            rows_ref[rows, section(k)] = both[:wide].astype(BF)
            tail = tail + both[wide:]
        rows_ref[rows, section(SECTIONS)] = tail.astype(BF)


def pack_blocks(rows_ref, block_ref):
    parts = halves(block_ref.shape[0])
    height = block_ref.shape[0] // parts
    wide = height // BLOCK * SLOTS
    r, i = iota((height, wide), 0), iota((height, wide), 1)
    peer, j = r >> 3, r & (BLOCK - 1)
    main = ((i == peer * SLOTS + j) & (j < SLOTS)).astype(F32).astype(BF)
    for g in range(parts):
        rows = slice(g * wide, (g + 1) * wide)
        tail = rows_ref[rows, section(SECTIONS)]
        for k in range(SECTIONS):
            last = ((i == peer * SLOTS + (j - SLOTS) * 3 + k) & (j >= SLOTS)).astype(F32).astype(BF)
            block_ref[g * height : (g + 1) * height, section(k)] = (
                dot(main, rows_ref[rows, section(k)]) + dot(last, tail)
            ).astype(BF)


def place_rows(shards, order_ref, target_ref, columns, sems, first):
    copies = []
    for n, shard in enumerate(shards):
        rows = pl.ds(pl.multiple_of(order_ref[n], LANES), shard.shape[0])
        copies.append(pltpu.make_async_copy(shard.at[:, columns], target_ref.at[rows], sems.at[first + n]))
    return copies


def forward_kernel(order_ref, block_ref, *refs):
    *shards, weights_hbm, down_hbm, factor_hbm, weights_ref, down_ref, factor_ref, rows_ref, sems = refs
    hidden, count = factor_ref.shape[1] // 2, len(shards)
    copies = place_rows(shards, order_ref, weights_ref, slice(0, 2 * hidden), sems, 0)
    down = place_rows(shards, order_ref, down_ref, slice(2 * hidden, 3 * hidden), sems, count)
    for copy in copies:
        copy.start()
    unpack_blocks(block_ref, rows_ref)
    for copy in down:
        copy.start()
    for copy in copies:
        copy.wait()
    keep = [
        pltpu.make_async_copy(source, target, sems.at[2 * count + n])
        for n, (source, target) in enumerate(
            ((weights_ref, weights_hbm), (down_ref, down_hbm), (factor_ref, factor_hbm))
        )
    ]
    keep[0].start()
    gate_pre = dot(rows_ref[...], weights_ref[:, :hidden])
    for copy in down:
        copy.wait()
    keep[1].start()
    up_pre = dot(rows_ref[...], weights_ref[:, hidden:])
    s = jax.nn.sigmoid(gate_pre)
    factor_ref[:, :hidden] = up_pre * s * (1.0 + gate_pre * (1.0 - s))
    factor_ref[:, hidden:] = gate_pre * s
    keep[2].start()
    for copy in keep:
        copy.wait()


def backward_kernel(
    block_hbm,
    weights_hbm,
    down_hbm,
    factor_hbm,
    out_ref,
    block_ref,
    weights_ref,
    down_ref,
    factor_ref,
    rows_ref,
    hidden_ref,
    sems,
):
    hidden = factor_ref.shape[1] // 2
    block, down, factor, weights = [
        pltpu.make_async_copy(source, target, sems.at[n])
        for n, (source, target) in enumerate(
            (
                (block_hbm, block_ref),
                (down_hbm, down_ref),
                (factor_hbm, factor_ref),
                (weights_hbm, weights_ref),
            )
        )
    ]
    block.start()
    down.start()
    block.wait()
    factor.start()
    weights.start()
    unpack_blocks(block_ref, rows_ref)
    down.wait()
    back = dot(rows_ref[...], down_ref[...])
    factor.wait()
    hidden_ref[:, :hidden] = (back * factor_ref[:, :hidden]).astype(BF)
    hidden_ref[:, hidden:] = (back * factor_ref[:, hidden:]).astype(BF)
    weights.wait()
    for k in range(SECTIONS + 1):
        rows_ref[:, section(k)] = dot_last(hidden_ref[...], weights_ref[section(k), :]).astype(BF)
    pack_blocks(rows_ref, out_ref)


def finish_kernel(
    block_ref, residual_ref, gain_ref, q_ref, units_ref, token_ref, out_ref, grad_ref
):
    total, q = block_ref.shape[0], q_ref[...]
    gates = units_ref[...].astype(F32) * (1.0 / 256.0)
    first, second = gates[0:1], gates[1:2]
    tokens = q.shape[1]
    main = picks(total, q, first, second)
    tail = jnp.zeros((tokens, SECTION), F32)
    for k in range(SECTIONS):
        both = dot_first(
            jnp.concatenate([main, picks(total, tail_row(q, k), first, second)], axis=1),
            block_ref[:, section(k)],
        )
        grad_ref[:, section(k)] = both[:tokens]
        tail = tail + both[tokens:]
    grad_ref[:, section(SECTIONS)] = tail
    stream = residual_ref[...].astype(F32)
    root = inverse_rms(stream)
    gain = gain_ref[...].astype(F32)
    for c in range(gain.shape[0]):
        lanes = slice(c * LANES, (c + 1) * LANES)
        grad_ref[:, lanes] = gain[c : c + 1] * grad_ref[:, lanes]
    scaled = grad_ref[...]
    correction = jnp.mean(scaled * stream, axis=-1, keepdims=True)
    cot = token_ref[...].astype(F32)
    out_ref[...] = (cot + root * scaled - stream * (root * root * root * correction)).astype(BF)


def params(mib):
    return pltpu.CompilerParams(vmem_limit_bytes=mib << 20)


IN_SMEM = pl.BlockSpec(memory_space=pltpu.SMEM)
IN_VMEM = pl.BlockSpec(memory_space=pltpu.VMEM)
IN_HBM = pl.BlockSpec(memory_space=pltpu.HBM)


def hbm(value):
    return pltpu.with_memory_space_constraint(value, pltpu.HBM)


def per_device(
    query_reps,
    code_reps,
    positives,
    file_lengths,
    residual,
    norm_gain,
    expert_ids,
    gate_units,
    w_gate,
    w_up,
    w_down,
):
    owners = lax.axis_size("expert")
    columns = code_reps.shape[0]
    queries, width = query_reps.shape
    files = file_lengths.shape[2]
    tokens = residual.shape[1]
    hidden = w_gate.shape[2]
    total = owners * BLOCK
    lengths = file_lengths.reshape(1, files)
    stream = residual[0]
    gain = norm_gain.reshape(width // LANES, LANES)
    ids = expert_ids[0].T
    units = gate_units[0].T

    owner = lax.axis_index("expert")[None]
    half = w_gate.shape[1] // 2

    def exchange(value):
        shape = value.shape
        return lax.all_to_all(
            value.reshape(owners, BLOCK, shape[1]), "expert", 0, 0, tiled=True
        ).reshape(shape)

    blocks, scores, q, local_top, local_rest, upper, lower = pl.pallas_call(
        functools.partial(dispatch_kernel, experts=owners),
        out_shape=(
            pltpu.HBM((total, BLOCK_WIDTH + LANES), BF),
            pltpu.HBM((columns, queries), F32),
            jax.ShapeDtypeStruct((2, tokens), jnp.int32),
            jax.ShapeDtypeStruct((1, queries), F32),
            jax.ShapeDtypeStruct((1, queries), F32),
            jax.ShapeDtypeStruct((half, 3 * hidden), BF),
            jax.ShapeDtypeStruct((half, 3 * hidden), BF),
        ),
        in_specs=[IN_SMEM] + [IN_HBM] * 9,
        out_specs=(IN_HBM, IN_HBM) + (IN_VMEM,) * 5,
        scratch_shapes=[
            pltpu.VMEM((2, tokens), jnp.int32),
            pltpu.VMEM((tokens, width), BF),
            pltpu.VMEM(gain.shape, BF),
            pltpu.VMEM((columns, width), BF),
            pltpu.VMEM((1, queries), jnp.int32),
            pltpu.VMEM((queries, width), BF),
            pltpu.VMEM((columns, queries), F32),
            pltpu.VMEM((tokens, width), BF),
            pltpu.VMEM((total, BLOCK_WIDTH + LANES), BF),
            pltpu.SemaphoreType.DMA((PIECES + 13 + SECTIONS,)),
        ],
        compiler_params=params(16),
        name="dispatch",
    )(
        owner,
        hbm(ids),
        hbm(stream),
        hbm(gain),
        hbm(code_reps),
        hbm(positives[None]),
        hbm(query_reps),
        hbm(w_gate[0]),
        hbm(w_up[0]),
        hbm(w_down[0]),
    )
    size = lax.axis_size("dp")
    me = lax.axis_index("dp")

    def ahead(value, step):
        return lax.ppermute(value, "dp", [(d, (d + step) % size) for d in range(size)])

    def partner(value):
        return lax.ppermute(value, "dp", [(d, d ^ 1) for d in range(size)])

    left, right = 2, size - 2
    upper_left, lower_right = ahead(upper, left), ahead(lower, right)
    lower_left, upper_right = ahead(lower, left), ahead(upper, right)
    partner_upper, partner_lower = partner(upper), partner(lower)
    partner_upper_left, partner_upper_right = partner(upper_left), partner(upper_right)
    moved = [upper_left, lower_right, lower_left, upper_right, partner_upper, partner_lower]
    moved += [partner_upper_left, partner_upper_right]
    blocks = exchange(blocks)
    parts = pl.pallas_call(
        weights_kernel,
        out_shape=jax.ShapeDtypeStruct((columns, width), BF),
        in_specs=[IN_VMEM, IN_SMEM] + [IN_VMEM] * 3 + [IN_HBM] * (2 + len(moved)),
        out_specs=IN_VMEM,
        scratch_shapes=[
            pltpu.VMEM((total, LANES), F32),
            pltpu.VMEM((columns, queries), BF),
            pltpu.VMEM((columns, queries), F32),
            pltpu.VMEM((queries, width), BF),
            pltpu.SemaphoreType.DMA((PIECES + 1,)),
        ],
        compiler_params=params(12),
        name="code_weights",
    )(
        blocks,
        owner,
        local_top,
        local_rest,
        positives[None],
        hbm(scores),
        hbm(query_reps),
        *[hbm(shard) for shard in moved],
    )
    parts = lax.all_to_all(
        parts.reshape(columns // files, files, width), "dp", 0, 0, tiled=True
    ).reshape(columns, width)
    cot_blocks, token_cot = pl.pallas_call(
        cotangent_kernel,
        out_shape=(
            pltpu.HBM((total, BLOCK_WIDTH), BF),
            pltpu.HBM((tokens, width), BF),
        ),
        in_specs=[IN_VMEM, IN_SMEM, IN_VMEM],
        out_specs=(IN_HBM, IN_HBM),
        scratch_shapes=[
            pltpu.VMEM((tokens, width), BF),
            pltpu.VMEM((total, BLOCK_WIDTH), BF),
            pltpu.SemaphoreType.DMA((SECTIONS + 1,)),
        ],
        compiler_params=params(12),
        name="cotangent",
    )(parts, lengths, q)
    cot_blocks = exchange(cot_blocks)
    moved = lax.optimization_barrier((*moved, parts))[:-1]
    upper_left, lower_right, lower_left, upper_right, partner_upper, partner_lower = moved[:6]
    partner_upper_left, partner_upper_right = moved[6:]
    upper_across, lower_across = ahead(upper_left, left), ahead(lower_right, right)
    shards = [upper, lower, partner_upper, partner_lower]
    shards += [upper_left, lower_left, upper_right, lower_right, upper_across, lower_across]
    shards += [partner_upper_left, partner(lower_left), partner_upper_right, partner(lower_right)]
    shards += [partner(upper_across), partner(lower_across)]
    shards = [hbm(shard) for shard in shards]
    places = [(d, 0, start) for d in (me, me ^ 1) for start in (0, half)]
    places += [
        (d, step, start) for d in (me, me ^ 1) for step in (size - 2, 2, 4) for start in (0, half)
    ]
    order = jnp.stack(
        [jnp.bitwise_and(d + step, size - 1) * (2 * half) + start for d, step, start in places]
    ).astype(jnp.int32)

    rows = owners * SLOTS
    weights, down, factor = pl.pallas_call(
        forward_kernel,
        out_shape=(
            pltpu.HBM((width, 2 * hidden), BF),
            pltpu.HBM((width, hidden), BF),
            pltpu.HBM((rows, 2 * hidden), F32),
        ),
        in_specs=[IN_SMEM, IN_VMEM] + [IN_HBM] * len(shards),
        out_specs=(IN_HBM,) * 3,
        scratch_shapes=[
            pltpu.VMEM((width, 2 * hidden), BF),
            pltpu.VMEM((width, hidden), BF),
            pltpu.VMEM((rows, 2 * hidden), F32),
            pltpu.VMEM((rows, width), BF),
            pltpu.SemaphoreType.DMA((2 * len(shards) + 3,)),
        ],
        compiler_params=params(32),
        name="expert_forward",
    )(order, blocks, *shards)
    result = pl.pallas_call(
        backward_kernel,
        out_shape=jax.ShapeDtypeStruct((total, BLOCK_WIDTH), BF),
        in_specs=[IN_HBM] * 4,
        out_specs=IN_VMEM,
        scratch_shapes=[
            pltpu.VMEM((total, BLOCK_WIDTH), BF),
            pltpu.VMEM((width, 2 * hidden), BF),
            pltpu.VMEM((width, hidden), BF),
            pltpu.VMEM((rows, 2 * hidden), F32),
            pltpu.VMEM((rows, width), BF),
            pltpu.VMEM((rows, 2 * hidden), BF),
            pltpu.SemaphoreType.DMA((4,)),
        ],
        compiler_params=params(32),
        name="expert_backward",
    )(hbm(cot_blocks), hbm(weights), hbm(down), hbm(factor))

    token_grad = pl.pallas_call(
        finish_kernel,
        out_shape=jax.ShapeDtypeStruct((tokens, width), BF),
        in_specs=[IN_VMEM] * 6,
        out_specs=IN_VMEM,
        scratch_shapes=[pltpu.VMEM((tokens, width), F32)],
        compiler_params=params(12),
        name="finish",
    )(exchange(result), stream, gain, q, units, token_cot)
    return token_grad[None]


def solution(mesh):
    return jax.shard_map(
        per_device,
        mesh=mesh,
        in_specs=(
            P("dp", None),
            P("expert", None),
            P("dp"),
            P("expert", "dp", None),
            P("expert", "dp", None),
            P(),
            P("expert", "dp", None),
            P("expert", "dp", None),
            P("expert", "dp", None),
            P("expert", "dp", None),
            P("expert", "dp", None),
        ),
        out_specs=P("expert", "dp", None),
        check_vma=False,
    )
```
